256 devices in a mesh: grp: 8 (over z), ep: 16 (over x, y), tp: 2 (over core).
Axes of the slice: x: 4, y: 4, z: 8, core: 2. Of those that a mesh axis runs over, the one named last changes fastest.
Arguments:
- tokens: bfloat16 [16384, 2048], P(('grp', 'ep'), 'tp'), may hold values from -6 to 6
- expert_ids: int32 [16384, 4], P(('grp', 'ep')), may hold values from 0 to 127, all different within a row; in each aligned block of 128 rows (0 to 127, 128 to 255, ...) at most 6 rows name the same one
- router_probs: float32 [16384, 4], P(('grp', 'ep')), may hold values from 0.02 to 1
- cotangent: bfloat16 [16384, 2048], P(('grp', 'ep'), 'tp'), may hold values from -6 to 6
- w_gate: bfloat16 [128, 2048, 768], P(('grp', 'ep'), None, 'tp'), may hold values from -0.125 to 0.125
- w_up: bfloat16 [128, 2048, 768], P(('grp', 'ep'), None, 'tp'), may hold values from -0.125 to 0.125
- w_down: bfloat16 [128, 768, 2048], P(('grp', 'ep'), 'tp'), may hold values from -0.21875 to 0.21875
Outputs:
- layer_out: bfloat16 [16384, 2048], P(('grp', 'ep'), 'tp')
- grad_tokens: bfloat16 [16384, 2048], P(('grp', 'ep'), 'tp')
- grad_gate: bfloat16 [128, 2048, 768], P(('grp', 'ep'), None, 'tp')
- grad_up: bfloat16 [128, 2048, 768], P(('grp', 'ep'), None, 'tp')
- grad_down: bfloat16 [128, 768, 2048], P(('grp', 'ep'), 'tp')
The draws below stay inside these ranges and needn't reach their ends.
Inputs may be any that keep to these rules, and one draw needn't show every extreme that they name: `expert_ids`: each token names 4 different experts. Among the 128 rows of one index of grp+ep no expert is named by more than 6 tokens, and in some such block one expert is named by exactly 6.
All inputs are finite; a program needn't handle non-finite values.
Results may differ from the reference program's by a relative error of at most 0.0085.
Values may be sent and summed in bfloat16 or wider, within the bound.
No kernel may reach another device: no remote copies, remote signals or barrier semaphores. Data moves between devices by JAX's collectives and lax.ppermute only.
A program may use at most 128 MiB of HBM per device.

```python
import math
import jax
import jax.numpy as jnp
import numpy as np
from jax import lax

D = 2048
FF = 768
TOK_DEV = 128
TOPK = 4
EXPERTS = 128
CAP = 6
SLOTS = 768
TOKENS = 16384


def levels(own_key, shape, split, least, largest):
    gain, own = 1.0, jax.random.fold_in(own_key, 6)
    for axis_at, shards_of in split:
        heights = jnp.exp(jax.random.uniform(jax.random.fold_in(own, axis_at), (shards_of,), jnp.float32, least / len(split), largest / len(split)))
        gain = gain * jnp.repeat(heights, shape[axis_at] // shards_of).reshape([-1 if axis == axis_at else 1 for axis in range(len(shape))])
    return gain


def assign_block(stream_key, own, number, rows, count, top, reach, slope):
    ranking = jax.random.permutation(stream_key, count)
    crowded, common = shares(count, rows * top, reach, slope, True), shares(count, rows * top, reach, slope, False)
    places = jnp.arange(count)

    def named(tallies, turn):
        used = int((tallies > 0).sum())
        fixed = max(1, used // 4)
        shifted = fixed + (places - fixed + turn * (used - fixed)) % max(1, count - fixed)
        return jnp.zeros((count,), jnp.int32).at[ranking[jnp.where(places < fixed, places, shifted)]].set(jnp.asarray(tallies, jnp.int32))

    tallies = jnp.where(number % 4 == 0, named(crowded, number // 4), named(common, number - number // 4 - 1))
    mixed = jax.random.permutation(jax.random.fold_in(own, 3), count)
    donor, receiver = mixed[0:count // 2 * 2:2], mixed[1:count // 2 * 2:2]
    room = jnp.minimum(tallies[donor] - 1, reach - tallies[receiver]) // 2
    room = jnp.where((donor == ranking[0]) | (receiver == ranking[0]) | (tallies[receiver] == 0), 0, jnp.maximum(room, 0))
    shifted = jax.random.randint(jax.random.fold_in(own, 4), (count // 2,), 0, 1 << 20) % (room + 1)
    tallies = tallies.at[donor].add(-shifted).at[receiver].add(shifted)
    members = jnp.searchsorted(jnp.cumsum(tallies), jnp.arange(rows * top), side="right").astype(jnp.int32)
    listing = members.reshape(top, rows).T
    listing = listing[jax.random.permutation(jax.random.fold_in(own, 1), rows)]
    turn = jax.random.randint(jax.random.fold_in(own, 2), (rows, 1), 0, top)
    return jnp.take_along_axis(listing, (jnp.arange(top)[None, :] + turn) % top, axis=1)


def shares(count, total, limit, skew, full):
    loads = [(1 << 20) // math.isqrt(rank ** skew) + 1 for rank in range(1, count + 1)]
    largest = limit if full else min(limit, max(-(-total // count), total * loads[0] // sum(loads)))
    least = 1 if total - largest >= count - 1 else 0
    given, rest = [largest] + [least] * (count - 1), total - largest - least * (count - 1)
    while rest > 0:
        movable = [i for i in range(1, count) if given[i] < largest] or [i for i in range(1, count) if given[i] < limit]
        whole, left = sum([loads[i] for i in movable]), rest
        for i in movable:
            addition = min(limit - given[i], max(1, left * loads[i] // whole), rest)
            given[i] = given[i] + addition
            rest = rest - addition
    return np.array(given)


def centred(own_key, dims, width, most, split=(), kind=jnp.bfloat16):
    gain = levels(own_key, dims, split, -0.22, 0.18) if split else 1.0
    result = jax.random.normal(own_key, dims, jnp.float32) * width * gain
    return jnp.minimum(jnp.maximum(result, -most), most).astype(kind)


def setup_inputs(seed: int = 0) -> dict:
    arg_keys = jax.random.split(jax.random.key(seed), 8)
    tokens = centred(arg_keys[0], (TOKENS, D), 1.0, 6.0, ((0, 128), (1, 2)))
    expert_ids_keys = jax.random.split(jax.random.fold_in(arg_keys[1], 1), TOKENS // TOK_DEV)
    expert_ids_turns = jax.random.permutation(jax.random.fold_in(arg_keys[1], 3), TOKENS // TOK_DEV)
    expert_ids = jax.vmap(lambda own, number: assign_block(jax.random.fold_in(arg_keys[1], 2), own, number, TOK_DEV, EXPERTS, TOPK, CAP, 2))(expert_ids_keys, expert_ids_turns).reshape((TOKENS, TOPK))
    router_probs = jnp.clip(jnp.exp(math.log(1.0) - 3.912023 * jax.random.uniform(arg_keys[2], (TOKENS, TOPK), jnp.float32) ** levels(arg_keys[2], (TOKENS, TOPK), ((0, 128),), -0.2, 0.2)), 0.02, 1.0)
    cotangent = centred(arg_keys[3], (TOKENS, D), 1.0, 6.0, ((0, 128), (1, 2)))
    w_gate = centred(arg_keys[4], (EXPERTS, D, FF), D ** -0.5, 0.125, ((0, 128), (2, 2)))
    w_up = centred(arg_keys[5], (EXPERTS, D, FF), D ** -0.5, 0.125, ((0, 128), (2, 2)))
    w_down = centred(arg_keys[6], (EXPERTS, FF, D), FF ** -0.5, 0.21875, ((0, 128), (1, 2)))
    return {"tokens": tokens, "expert_ids": expert_ids, "router_probs": router_probs, "cotangent": cotangent, "w_gate": w_gate, "w_up": w_up, "w_down": w_down}


def reference(tokens, expert_ids, router_probs, cotangent, w_gate, w_up, w_down):
    combine = router_probs / jnp.sum(router_probs, axis=1, keepdims=True)
    flat_ids = expert_ids.reshape(-1)
    flat_weight = combine.reshape(-1)
    flat_token = (jnp.arange(TOKENS * TOPK) // TOPK).astype(jnp.int32)
    places = jnp.arange(SLOTS).astype(jnp.int32)

    def per_expert(carry, expert):
        out_total, grad_total = carry
        matches = flat_ids == expert
        where_rows = jnp.nonzero(matches, size=SLOTS, fill_value=0)[0].astype(jnp.int32)
        is_live = (places < jnp.sum(matches.astype(jnp.int32)).astype(jnp.int32)).astype(jnp.float32)
        token_rows = flat_token[where_rows]
        row_weight = flat_weight[where_rows] * is_live
        inputs = tokens[token_rows]
        gate_pre = jnp.dot(inputs, w_gate[expert], preferred_element_type=jnp.float32)
        up_pre = jnp.dot(inputs, w_up[expert], preferred_element_type=jnp.float32)
        sigmoid_gate = jax.nn.sigmoid(gate_pre)
        activated = gate_pre * sigmoid_gate
        hidden = (activated * up_pre).astype(jnp.bfloat16)
        expert_out = jnp.dot(hidden, w_down[expert], preferred_element_type=jnp.float32).astype(jnp.bfloat16)
        grad_row = (row_weight[:, None] * cotangent[token_rows].astype(jnp.float32)).astype(jnp.bfloat16)
        grad_hidden = jnp.dot(grad_row, w_down[expert].T, preferred_element_type=jnp.float32)
        grad_gate_pre = (grad_hidden * up_pre * sigmoid_gate * (1.0 + gate_pre * (1.0 - sigmoid_gate))).astype(jnp.bfloat16)
        grad_up_pre = (grad_hidden * activated).astype(jnp.bfloat16)
        grad_down_e = jnp.dot(hidden.T, grad_row, preferred_element_type=jnp.float32).astype(jnp.bfloat16)
        grad_gate_e = jnp.dot(inputs.T, grad_gate_pre, preferred_element_type=jnp.float32).astype(jnp.bfloat16)
        grad_up_e = jnp.dot(inputs.T, grad_up_pre, preferred_element_type=jnp.float32).astype(jnp.bfloat16)
        grad_row_in = (jnp.dot(grad_gate_pre, w_gate[expert].T, preferred_element_type=jnp.float32)
                       + jnp.dot(grad_up_pre, w_up[expert].T, preferred_element_type=jnp.float32)).astype(jnp.bfloat16)
        out_total = out_total.at[token_rows].add(row_weight[:, None] * expert_out.astype(jnp.float32))
        grad_total = grad_total.at[token_rows].add(is_live[:, None] * grad_row_in.astype(jnp.float32))
        return (out_total, grad_total), (grad_gate_e, grad_up_e, grad_down_e)

    start = (jnp.zeros((TOKENS, D), jnp.float32), jnp.zeros((TOKENS, D), jnp.float32))
    expert_list = jnp.arange(EXPERTS).astype(jnp.int32)
    (out_total, grad_total), (grad_gate, grad_up, grad_down) = lax.scan(per_expert, start, expert_list)
    return (out_total.astype(jnp.bfloat16), grad_total.astype(jnp.bfloat16), grad_gate, grad_up, grad_down)
```

```python
import jax
import jax.numpy as jnp
from jax import lax
from jax.sharding import PartitionSpec as P

PLANE = ("ep", "tp")


def shift(value, axis, distance):
    count = lax.axis_size(axis)
    return lax.ppermute(value, axis, [(i, (i + distance) % count) for i in range(count)])


def ring_offsets(count):
    order = [0]
    for step in range(1, count // 2):
        order += [-step, step]
    return order + [count // 2]


def ring_gather(block, axis):
    count = lax.axis_size(axis)
    half = block.shape[0] // 2
    pieces, ahead, behind = [block], block, block
    for _ in range(1, count // 2):
        ahead, behind = shift(ahead, axis, 1), shift(behind, axis, -1)
        pieces += [ahead, behind]
    pieces += [shift(ahead[:half], axis, 1), shift(behind[half:], axis, -1)]
    return jnp.concatenate(pieces, axis=0)


def add_rounded(first, second):
    return (first.astype(jnp.float32) + second.astype(jnp.float32)).astype(jnp.bfloat16)


def ring_scatter(blocks, axis):
    count = lax.axis_size(axis)
    half = blocks[0].shape[0] // 2
    where = {offset: i for i, offset in enumerate(ring_offsets(count))}
    far = blocks[where[count // 2]]
    down, up = shift(far[:half], axis, -1), shift(far[half:], axis, 1)
    for step in range(count // 2 - 1, 0, -1):
        lower, upper = blocks[where[-step]], blocks[where[step]]
        if step == count // 2 - 1:
            down = jnp.concatenate([add_rounded(lower[:half], down), lower[half:]], axis=0)
            up = jnp.concatenate([upper[:half], add_rounded(upper[half:], up)], axis=0)
        else:
            down, up = add_rounded(lower, down), add_rounded(upper, up)
        down, up = shift(down, axis, -1), shift(up, axis, 1)
    total = blocks[0].astype(jnp.float32) + down.astype(jnp.float32) + up.astype(jnp.float32)
    return total.astype(jnp.bfloat16)


def contract(left, right, dims):
    return lax.dot_general(left, right, (dims, ((), ())), preferred_element_type=jnp.float32)


def on_device(tokens, expert_ids, router_probs, cotangent, w_gate, w_up, w_down):
    planes, columns, cores = lax.axis_size("grp"), lax.axis_size("ep"), lax.axis_size("tp")
    tok_rows, width = tokens.shape
    top_count = expert_ids.shape[1]
    capacity = 3 * tok_rows * top_count // (2 * planes * columns)
    me = lax.axis_index("grp")
    gathered = ring_gather(jnp.concatenate([tokens, cotangent], axis=1), "grp")

    combine = router_probs / jnp.sum(router_probs, axis=1, keepdims=True)
    routing = jnp.concatenate([expert_ids.T.astype(jnp.float32), combine.T], axis=0)
    routing = lax.all_gather(routing, "grp", axis=0, tiled=False)
    order = (me + jnp.array(ring_offsets(planes), jnp.int32) + planes) % planes
    routing = jnp.take(routing, order, axis=0)
    gate_full = lax.all_gather(w_gate[0], "tp", axis=1, tiled=True)
    up_full = lax.all_gather(w_up[0], "tp", axis=1, tiled=True)
    down_full = lax.all_gather(w_down[0], "tp", axis=0, tiled=True)

    local = routing[:, :top_count] - (me * columns).astype(jnp.float32)
    expert = jnp.arange(columns, dtype=jnp.float32)[:, None, None, None]
    hits = local[None] == expert
    named = jnp.any(hits, axis=2)
    weight = jnp.sum(jnp.where(hits, routing[None, :, top_count:], 0.0), axis=2)
    row_at = jnp.arange(tok_rows, dtype=jnp.int32)
    earlier = (row_at[:, None] < row_at[None, :]).astype(jnp.bfloat16)
    rank = contract(
        named.astype(jnp.bfloat16).reshape(columns * planes, tok_rows), earlier, ((1,), (0,))
    ).reshape(columns, planes, tok_rows)
    base = (jnp.arange(planes, dtype=jnp.float32) * capacity)[None, :, None]
    place = jnp.where(named, base + rank, -1.0).reshape(columns, 1, planes * tok_rows)
    weight = weight.reshape(columns, 1, planes * tok_rows)
    slot = jnp.arange(planes * capacity, dtype=jnp.float32)[None, :, None]
    chosen = place == slot
    slot_count = columns * planes * capacity
    select = chosen.astype(jnp.bfloat16).reshape(slot_count, planes * tok_rows)
    weighted = jnp.where(chosen, weight, 0.0)
    slot_weight = jnp.sum(weighted, axis=2).reshape(slot_count, 1)

    sent = contract(select, gathered, ((1,), (0,)))
    sent = jnp.concatenate([sent[:, :width], slot_weight * sent[:, width:]], axis=1).astype(jnp.bfloat16)
    arrived = lax.all_to_all(sent, PLANE, split_axis=0, concat_axis=0, tiled=True)
    group = slot_count // (columns * cores)
    rows_here = columns * group
    arrived = arrived.reshape(columns, cores, group, 2 * width)
    halves = [arrived[:, core].reshape(rows_here, 2 * width) for core in range(cores)]
    rows = jnp.concatenate([half[:, :width] for half in halves], axis=1)
    grads = jnp.concatenate([half[:, width:] for half in halves], axis=1)

    gate_pre = contract(rows, gate_full, ((1,), (0,)))
    up_pre = contract(rows, up_full, ((1,), (0,)))
    sigmoid_gate = jax.nn.sigmoid(gate_pre)
    activated = gate_pre * sigmoid_gate
    hidden = (activated * up_pre).astype(jnp.bfloat16)
    out = contract(hidden, down_full, ((1,), (0,))).astype(jnp.bfloat16)
    grad_hidden = contract(grads, down_full, ((1,), (1,)))
    grad_gate_pre = (
        grad_hidden * up_pre * sigmoid_gate * (1.0 + gate_pre * (1.0 - sigmoid_gate))
    ).astype(jnp.bfloat16)
    grad_up_pre = (grad_hidden * activated).astype(jnp.bfloat16)
    grad_in = (
        contract(grad_gate_pre, gate_full, ((1,), (1,))) + contract(grad_up_pre, up_full, ((1,), (1,)))
    ).astype(jnp.bfloat16)

    back = [
        jnp.concatenate([out[:, at : at + width], grad_in[:, at : at + width]], axis=1).reshape(columns, group, 2 * width)
        for at in range(0, cores * width, width)
    ]
    back = jnp.stack(back, axis=1).reshape(slot_count, 2 * width)
    returned = lax.all_to_all(back, PLANE, split_axis=0, concat_axis=0, tiled=True)

    hidden_half = grad_gate_pre.shape[1] // cores
    grad_down = contract(hidden, grads, ((0,), (0,))).astype(jnp.bfloat16)
    grad_down = lax.psum_scatter(grad_down, "tp", scatter_dimension=0, tiled=True)

    def in_halves(grad):
        parts = [
            contract(rows, grad[:, at : at + hidden_half], ((0,), (0,))).astype(jnp.bfloat16)
            for at in range(0, cores * hidden_half, hidden_half)
        ]
        return lax.psum_scatter(jnp.concatenate(parts, axis=0), "tp", scatter_dimension=0, tiled=True)

    grad_gate, grad_up = in_halves(grad_gate_pre), in_halves(grad_up_pre)

    slots_each = planes * capacity
    spread = (jnp.arange(columns)[:, None] == jnp.arange(slot_count)[None, :] // slots_each).astype(jnp.bfloat16)
    place_wide = contract(place.reshape(columns, -1).T.astype(jnp.bfloat16), spread, ((1,), (0,)))
    weight_wide = contract(weight.reshape(columns, -1).T.astype(jnp.bfloat16), spread, ((1,), (0,)))
    chosen_back = place_wide == (jnp.arange(slot_count) % slots_each).astype(jnp.float32)[None, :]
    gather_in = chosen_back.astype(jnp.bfloat16)
    gather_out = jnp.where(chosen_back, weight_wide, 0.0).astype(jnp.bfloat16)
    gather_in, gather_out = lax.optimization_barrier((gather_in, gather_out))
    part_out = contract(gather_out, returned[:, :width], ((1,), (0,)))
    part_in = contract(gather_in, returned[:, width:], ((1,), (0,)))
    parts = jnp.concatenate([part_out, part_in], axis=1).astype(jnp.bfloat16)
    blocks = [parts[i * tok_rows : (i + 1) * tok_rows] for i in range(planes)]
    total = ring_scatter(blocks, "grp")
    return (total[:, :width], total[:, width:], grad_gate[None], grad_up[None], grad_down[None])


def solution(mesh):
    return jax.shard_map(
        on_device,
        mesh=mesh,
        in_specs=(
            P(("grp", "ep"), "tp"),
            P(("grp", "ep"), None),
            P(("grp", "ep"), None),
            P(("grp", "ep"), "tp"),
            P(("grp", "ep"), None, "tp"),
            P(("grp", "ep"), None, "tp"),
            P(("grp", "ep"), "tp", None),
        ),
        out_specs=(
            P(("grp", "ep"), "tp"),
            P(("grp", "ep"), "tp"),
            P(("grp", "ep"), None, "tp"),
            P(("grp", "ep"), None, "tp"),
            P(("grp", "ep"), "tp", None),
        ),
        check_vma=False,
    )
```

```python
import functools

import jax
import jax.numpy as jnp
from jax import lax
from jax.experimental import pallas as pl
from jax.experimental.pallas import tpu as pltpu
from jax.sharding import PartitionSpec as P

PLANE = ("ep", "tp")
VMEM = pl.BlockSpec(memory_space=pltpu.VMEM)
HBM = pl.BlockSpec(memory_space=pl.ANY)
SMALL, LARGE = 16 << 20, 40 << 20
CHUNK = 256


def shift(value, axis, distance):
    count = lax.axis_size(axis)
    return lax.ppermute(value, axis, [(i, (i + distance) % count) for i in range(count)])


def ring_offsets(count):
    order = [0]
    for step in range(1, count // 2):
        order += [-step, step]
    return order + [count // 2]


def ring_gather(block, axis, small=None):
    count = lax.axis_size(axis)
    half = block.shape[1] // 2
    pieces, ahead, behind = [block], block, block
    distance = 1
    for _ in range(1, count // 2):
        if small is not None and distance < count:
            moved = shift(small, axis, distance)
        ahead, behind = shift(ahead, axis, 1), shift(behind, axis, -1)
        pieces += [ahead, behind]
        if small is not None and distance < count:
            small = jnp.concatenate([small, moved], axis=0)
            small, ahead = lax.optimization_barrier((small, ahead))
            distance *= 2
    pieces += [shift(ahead[:, :half], axis, 1), shift(behind[:, half:], axis, -1)]
    return pieces if small is None else (pieces, small)


def add_rounded(first, second):
    return (first.astype(jnp.float32) + second.astype(jnp.float32)).astype(jnp.bfloat16)


def ring_scatter(blocks, far, axis):
    count = lax.axis_size(axis)
    half = blocks[0].shape[1] // 2
    where = {offset: i for i, offset in enumerate(ring_offsets(count))}
    down, up = shift(far[0], axis, -1), shift(far[1], axis, 1)
    for step in range(count // 2 - 1, 0, -1):
        lower, upper = blocks[where[-step]], blocks[where[step]]
        if step == count // 2 - 1:
            down = jnp.concatenate([add_rounded(lower[:, :half], down), lower[:, half:]], axis=1)
            up = jnp.concatenate([upper[:, :half], add_rounded(upper[:, half:], up)], axis=1)
        else:
            down, up = add_rounded(lower, down), add_rounded(upper, up)
        down, up = shift(down, axis, -1), shift(up, axis, 1)
    return [
        sum(part[:, at : at + half].astype(jnp.float32) for part in (blocks[0], down, up)).astype(jnp.bfloat16)
        for at in (0, half)
    ]


def contract(left, right, dims):
    return lax.dot_general(left, right, (dims, ((), ())), preferred_element_type=jnp.float32)


def pick_kernel(select, weight, *refs):
    pieces, out = refs[:-1], refs[-1]
    columns, _, group, width = out.shape
    middle = width // 2
    each = (len(pieces) - 1) // select.shape[0]
    for half in range(select.shape[0]):
        for at in (0, middle):
            whole = [piece[:, at : at + middle] for piece in pieces[:-2]] + [pieces[-1 if at else -2][...]]
            source = jnp.concatenate(whole[half * each : (half + 1) * each], axis=0)
            picked = contract(select[half], source, ((1,), (0,)))
            if at:
                picked = picked * weight[half]
            out[:, half, :, at : at + middle] = picked.astype(out.dtype).reshape(columns, group, middle)


def pick(select, weight, pieces, shape):
    return pl.pallas_call(
        pick_kernel,
        out_shape=jax.ShapeDtypeStruct(shape, jnp.bfloat16),
        in_specs=[VMEM] * (2 + len(pieces)),
        out_specs=VMEM,
        compiler_params=pltpu.CompilerParams(vmem_limit_bytes=SMALL),
        name="pick",
    )(select, weight, *pieces)


def combine_kernel(gather_out, gather_in, returned, *outs):
    blocks, far = outs[:-2], outs[-2:]
    halves, tokens, middle = gather_out.shape[0], blocks[0].shape[0], blocks[0].shape[1] // 2
    each = (len(blocks) + 1) // halves
    for half in range(halves):
        for side, gather in enumerate((gather_out, gather_in)):
            columns = slice(side * middle, (side + 1) * middle)
            rows = returned[:, half, :, columns].reshape(gather.shape[2], middle)
            total = contract(gather[half], rows, ((1,), (0,))).astype(jnp.bfloat16)
            for i in range(each):
                part = total[i * tokens : (i + 1) * tokens]
                if half * each + i < len(blocks):
                    blocks[half * each + i][:, columns] = part
                else:
                    far[side][...] = part


def combine_rows(gather_out, gather_in, returned, tokens):
    halves, half_tokens, _ = gather_out.shape
    planes, width = halves * half_tokens // tokens, returned.shape[3]
    block = jax.ShapeDtypeStruct((tokens, width), jnp.bfloat16)
    far = jax.ShapeDtypeStruct((tokens, width // 2), jnp.bfloat16)
    outs = pl.pallas_call(
        combine_kernel,
        out_shape=[block] * (planes - 1) + [far] * 2,
        in_specs=[VMEM] * 3,
        out_specs=[VMEM] * (planes + 1),
        compiler_params=pltpu.CompilerParams(vmem_limit_bytes=SMALL),
        name="combine_rows",
    )(gather_out, gather_in, returned)
    return outs[:-2], outs[-2:]


def cost(flops, arrays):
    return pl.CostEstimate(flops=flops, transcendentals=0, bytes_accessed=sum(2 * a.size for a in arrays))


def chunks(total, body):
    def step(i, carry):
        body(pl.ds(pl.multiple_of(i * CHUNK, CHUNK), CHUNK))
        return carry

    lax.fori_loop(0, total // CHUNK, step, 0)


def join_cores(arrived, joined, side):
    width = arrived.shape[3] // 2
    for core in range(arrived.shape[1]):
        block = arrived[:, core, :, side * width : (side + 1) * width]
        joined[:, core * width : (core + 1) * width] = block.reshape(joined.shape[0], width)


def split_cores(whole, out, side):
    width = out.shape[3] // 2
    for core in range(out.shape[1]):
        block = whole[:, core * width : (core + 1) * width].reshape(out.shape[0], out.shape[2], width)
        out[:, core, :, side * width : (side + 1) * width] = block


def expert_kernel(arrived, *refs):
    sources, (inner, out, rows, grads, gate_pre, up_pre, whole, gate_in, up_in, down_in, sems) = refs[:6], refs[6:]
    width = gate_in.shape[1] // 2
    own, other = slice(0, width), slice(width, 2 * width)
    targets = [
        gate_in.at[:, own], gate_in.at[:, other], up_in.at[:, own], up_in.at[:, other], down_in.at[own], down_in.at[other]
    ]
    copies = [
        pltpu.make_async_copy(source, target, sems.at[i])
        for i, (source, target) in enumerate(zip(sources, targets, strict=True))
    ]
    for copy in copies:
        copy.start()
    join_cores(arrived, rows, 0)
    join_cores(arrived, grads, 1)
    copies[0].wait()
    copies[1].wait()

    def gate_part(at):
        gate_pre[:, at] = contract(rows[...], gate_in[:, at], ((1,), (0,)))

    chunks(gate_pre.shape[1], gate_part)
    copies[2].wait()
    copies[3].wait()

    def up_part(at):
        up_at = contract(rows[...], up_in[:, at], ((1,), (0,)))
        up_pre[:, at] = up_at
        gate_at = gate_pre[:, at]
        inner[0, :, at] = (gate_at * jax.nn.sigmoid(gate_at) * up_at).astype(inner.dtype)

    chunks(up_pre.shape[1], up_part)
    copies[4].wait()
    copies[5].wait()

    def out_part(at):
        whole[:, at] = contract(inner[0], down_in[:, at], ((1,), (0,))).astype(whole.dtype)

    chunks(whole.shape[1], out_part)
    split_cores(whole, out, 0)

    def hidden_part(at):
        grad_hidden = contract(grads[...], down_in[at, :], ((1,), (1,)))
        gate_at = gate_pre[:, at]
        sigmoid_gate = jax.nn.sigmoid(gate_at)
        inner[1, :, at] = (
            grad_hidden * up_pre[:, at] * sigmoid_gate * (1.0 + gate_at * (1.0 - sigmoid_gate))
        ).astype(inner.dtype)
        inner[2, :, at] = (grad_hidden * (gate_at * sigmoid_gate)).astype(inner.dtype)

    chunks(gate_pre.shape[1], hidden_part)

    def in_part(at):
        total = contract(inner[1], gate_in[at, :], ((1,), (1,)))
        total = total + contract(inner[2], up_in[at, :], ((1,), (1,)))
        whole[:, at] = total.astype(whole.dtype)

    chunks(whole.shape[1], in_part)
    split_cores(whole, out, 1)


def expert(arrived, gate, up, down):
    columns, cores, group, width = arrived.shape
    count, hidden, features = columns * group, cores * gate[0].shape[1], gate[0].shape[0]
    rows, pre = pltpu.VMEM((count, features), jnp.bfloat16), pltpu.VMEM((count, hidden), jnp.float32)
    side = pltpu.VMEM((features, hidden), jnp.bfloat16)
    return pl.pallas_call(
        expert_kernel,
        out_shape=[
            jax.ShapeDtypeStruct((3, count, hidden), jnp.bfloat16),
            jax.ShapeDtypeStruct(arrived.shape, jnp.bfloat16),
        ],
        in_specs=[VMEM] + [HBM] * 6,
        out_specs=[VMEM] * 2,
        scratch_shapes=[
            rows, rows, pre, pre, rows, side, side,
            pltpu.VMEM((hidden, features), jnp.bfloat16), pltpu.SemaphoreType.DMA((6,)),
        ],
        compiler_params=pltpu.CompilerParams(vmem_limit_bytes=LARGE),
        cost_estimate=cost(12 * count * hidden * features, [*gate, *up, *down]),
        name="expert",
    )(arrived, *gate, *up, *down)


def weights_kernel(arrived, arrived_other, inner, inner_other, gate_out, up_out, down_out, rows, grads, hidden):
    count, width = inner.shape[1], inner.shape[2] // 2
    for core, block in enumerate((arrived, arrived_other)):
        at = slice(core * count, (core + 1) * count)
        join_cores(block, rows.at[at], 0)
        join_cores(block, grads.at[at], 1)
        for i in range(inner.shape[0]):
            hidden[i, at] = inner_other[i] if core else inner[i, :, :width]

    def by_feature(at):
        part = rows[:, at]
        gate_out[at, :] = contract(part, hidden[1], ((0,), (0,))).astype(gate_out.dtype)
        up_out[at, :] = contract(part, hidden[2], ((0,), (0,))).astype(up_out.dtype)
        down_out[:, at] = contract(hidden[0], grads[:, at], ((0,), (0,))).astype(down_out.dtype)

    chunks(rows.shape[1], by_feature)


def weight_grads(arrived, arrived_other, inner, inner_other):
    columns, cores, group, width = arrived.shape
    count, features, hidden = columns * group, cores * width // 2, inner.shape[2] // 2
    side = jax.ShapeDtypeStruct((features, hidden), jnp.bfloat16)
    rows = pltpu.VMEM((2 * count, features), jnp.bfloat16)
    return pl.pallas_call(
        weights_kernel,
        out_shape=[side, side, jax.ShapeDtypeStruct((hidden, features), jnp.bfloat16)],
        in_specs=[VMEM] * 4,
        out_specs=[VMEM] * 3,
        scratch_shapes=[rows, rows, pltpu.VMEM((3, 2 * count, hidden), jnp.bfloat16)],
        compiler_params=pltpu.CompilerParams(vmem_limit_bytes=LARGE),
        cost_estimate=cost(12 * count * hidden * features, [side, side, side]),
        name="weight_grads",
    )(arrived, arrived_other, inner, inner_other)


def on_device(tokens, expert_ids, router_probs, cotangent, w_gate, w_up, w_down):
    planes, columns, cores = lax.axis_size("grp"), lax.axis_size("ep"), lax.axis_size("tp")
    tok_rows, width = tokens.shape
    top_count = expert_ids.shape[1]
    capacity = 3 * tok_rows * top_count // (2 * planes * columns)
    group = planes * capacity // cores
    half_tokens = planes * tok_rows // cores
    me = lax.axis_index("grp")

    combine = router_probs / jnp.sum(router_probs, axis=1, keepdims=True)
    routing = jnp.concatenate([expert_ids.T.astype(jnp.float32), combine.T], axis=0)
    pieces, routing = ring_gather(jnp.concatenate([tokens, cotangent], axis=1), "grp", routing[None])
    routing = jnp.stack([routing[-offset % planes] for offset in ring_offsets(planes)])

    local = routing[:, :top_count] - (me * columns).astype(jnp.float32)
    plane_expert = jnp.arange(columns, dtype=jnp.float32)[:, None, None, None]
    hits = local[None] == plane_expert
    named = jnp.any(hits, axis=2)
    weight = jnp.sum(jnp.where(hits, routing[None, :, top_count:], 0.0), axis=2)
    row_at = jnp.arange(tok_rows, dtype=jnp.int32)
    earlier = (row_at[:, None] < row_at[None, :]).astype(jnp.bfloat16)
    rank = contract(
        named.astype(jnp.bfloat16).reshape(columns * planes, tok_rows), earlier, ((1,), (0,))
    ).reshape(columns, planes, tok_rows)
    base = ((jnp.arange(planes) % (planes // cores)) * capacity).astype(jnp.float32)[None, :, None]
    place = jnp.where(named, base + rank, -1.0).reshape(columns, cores, half_tokens)
    weight = weight.reshape(columns, cores, half_tokens)
    slot = jnp.arange(group, dtype=jnp.float32)[None, None, :, None]
    chosen = place.transpose(1, 0, 2)[:, :, None, :] == slot
    select = chosen.astype(jnp.bfloat16).reshape(cores, columns * group, half_tokens)
    slot_weight = jnp.sum(jnp.where(chosen, weight.transpose(1, 0, 2)[:, :, None, :], 0.0), axis=3)
    slot_weight = slot_weight.reshape(cores, columns * group, 1)

    spread = (jnp.arange(columns)[:, None] == jnp.arange(columns * group)[None, :] // group).astype(jnp.bfloat16)
    place_wide = contract(place.transpose(1, 2, 0).astype(jnp.bfloat16), spread, ((2,), (0,)))
    weight_wide = contract(weight.transpose(1, 2, 0).astype(jnp.bfloat16), spread, ((2,), (0,)))
    chosen_back = place_wide == (jnp.arange(columns * group) % group).astype(jnp.float32)[None, None, :]
    gather_in = chosen_back.astype(jnp.bfloat16)
    gather_out = jnp.where(chosen_back, weight_wide, 0.0).astype(jnp.bfloat16)

    shape = (columns, cores, group, 2 * width)

    def exchange(block):
        flat = block.reshape(columns * cores * group, 2 * width)
        return lax.all_to_all(flat, PLANE, split_axis=0, concat_axis=0, tiled=True).reshape(shape)

    def pair(block):
        return block, shift(block, "tp", 1)

    arrived = exchange(pick(select, slot_weight, pieces, shape))
    inner, back = expert(arrived, pair(w_gate[0]), pair(w_up[0]), pair(w_down[0]))
    returned = exchange(back)
    inner_other = shift(inner[:, :, inner.shape[2] // 2 :], "tp", 1)
    weights = weight_grads(*pair(arrived), inner, inner_other)
    returned, grad_gate, grad_up, grad_down = lax.optimization_barrier((returned, *weights))
    layer_out, grad_tokens = ring_scatter(*combine_rows(gather_out, gather_in, returned, tok_rows), "grp")
    return (layer_out, grad_tokens, grad_gate[None], grad_up[None], grad_down[None])


def solution(mesh):
    return jax.shard_map(
        on_device,
        mesh=mesh,
        in_specs=(
            P(("grp", "ep"), "tp"),
            P(("grp", "ep"), None),
            P(("grp", "ep"), None),
            P(("grp", "ep"), "tp"),
            P(("grp", "ep"), None, "tp"),
            P(("grp", "ep"), None, "tp"),
            P(("grp", "ep"), "tp", None),
        ),
        out_specs=(
            P(("grp", "ep"), "tp"),
            P(("grp", "ep"), "tp"),
            P(("grp", "ep"), None, "tp"),
            P(("grp", "ep"), None, "tp"),
            P(("grp", "ep"), "tp", None),
        ),
        check_vma=False,
    )
```

```python
import functools

import jax
import jax.numpy as jnp
from jax import lax
from jax.experimental import pallas as pl
from jax.experimental.pallas import tpu as pltpu
from jax.sharding import PartitionSpec as P

PLANE = ("ep", "tp")
VMEM = pl.BlockSpec(memory_space=pltpu.VMEM)
HBM = pl.BlockSpec(memory_space=pl.ANY)
SMALL, MIDDLE, LARGE = 16 << 20, 28 << 20, 56 << 20
CHUNK = 256


def shift(value, axis, distance):
    count = lax.axis_size(axis)
    return lax.ppermute(value, axis, [(i, (i + distance) % count) for i in range(count)])


def ring_offsets(count):
    order = [0]
    for step in range(1, count // 2):
        order += [-step, step]
    return order + [count // 2]


def ring_gathers(blocks, axis, small):
    count = lax.axis_size(axis)
    pieces = [[block] for block in blocks]
    ahead, behind = list(blocks), list(blocks)
    distance = 1
    for _ in range(1, count // 2):
        if distance < count:
            moved = shift(small, axis, distance)
        for i in range(len(blocks)):
            ahead[i], behind[i] = shift(ahead[i], axis, 1), shift(behind[i], axis, -1)
            pieces[i] += [ahead[i], behind[i]]
        if distance < count:
            small = jnp.concatenate([small, moved], axis=0)
            small, ahead[0] = lax.optimization_barrier((small, ahead[0]))
            distance *= 2
    pieces[0].append(shift(ahead[0], axis, 1))
    pieces[1].append(shift(behind[1], axis, -1))
    return pieces[0] + pieces[1], small


def add_rounded(first, second):
    return (first.astype(jnp.float32) + second.astype(jnp.float32)).astype(jnp.bfloat16)


def ring_scatter(blocks, axis, side):
    count = lax.axis_size(axis)
    where = {offset: i for i, offset in enumerate(ring_offsets(count))}
    sums = [None, None]
    sums[side] = shift(blocks[-1], axis, 1 if side else -1)
    for step in range(count // 2 - 1, 0, -1):
        for way, sign in enumerate((-1, 1)):
            mine = blocks[where[sign * step]]
            total = mine if sums[way] is None else add_rounded(mine, sums[way])
            sums[way] = shift(total, axis, sign)
    return sum(part.astype(jnp.float32) for part in (blocks[0], *sums)).astype(jnp.bfloat16)


def contract(left, right, dims):
    return lax.dot_general(left, right, (dims, ((), ())), preferred_element_type=jnp.float32)


def pick_kernel(select, weight, *refs):
    pieces, (sent, out, sems) = refs[:-3], refs[-3:]
    columns, _, group, width = out.shape
    middle, count = width // 2, len(pieces) // 2
    each, copies = count // select.shape[0], []
    for side in (0, 1):
        whole = [piece[...] for piece in pieces[side * count : (side + 1) * count]]
        for half in range(select.shape[0]):
            source = jnp.concatenate(whole[half * each : (half + 1) * each], axis=0)
            picked = contract(select[half], source, ((1,), (0,)))
            if side:
                picked = picked * weight[half]
            at = slice(side * middle, (side + 1) * middle)
            out[:, half, :, at] = picked.astype(out.dtype).reshape(columns, group, middle)
            copies.append(
                pltpu.make_async_copy(out.at[:, half, :, at], sent.at[:, half, :, at], sems.at[2 * side + half])
            )
            copies[-1].start()
    for copy in copies:
        copy.wait()


def pick(select, weight, pieces, shape):
    return pl.pallas_call(
        pick_kernel,
        out_shape=jax.ShapeDtypeStruct(shape, jnp.bfloat16),
        in_specs=[VMEM] * (2 + len(pieces)),
        out_specs=HBM,
        scratch_shapes=[pltpu.VMEM(shape, jnp.bfloat16), pltpu.SemaphoreType.DMA((4,))],
        compiler_params=pltpu.CompilerParams(vmem_limit_bytes=SMALL),
        name="pick",
    )(select, weight, *pieces)


def combine_kernel(gather_out, gather_in, returned, *outs):
    halves, middle = gather_out.shape[0], returned.shape[3] // 2
    count = len(outs) // 2
    tokens, each = outs[0].shape[0], count // halves
    for side, gather in enumerate((gather_out, gather_in)):
        blocks = outs[side * count : (side + 1) * count]
        for half in range(halves):
            rows = returned[:, half, :, side * middle : (side + 1) * middle].reshape(gather.shape[2], middle)
            total = contract(gather[half], rows, ((1,), (0,))).astype(jnp.bfloat16)
            for i in range(each):
                blocks[half * each + i][...] = total[i * tokens : (i + 1) * tokens]


def combine_rows(gather_out, gather_in, returned, tokens):
    halves, half_tokens, _ = gather_out.shape
    planes, width = halves * half_tokens // tokens, returned.shape[3] // 2
    block = jax.ShapeDtypeStruct((tokens, width), jnp.bfloat16)
    outs = pl.pallas_call(
        combine_kernel,
        out_shape=[block] * (2 * planes),
        in_specs=[VMEM] * 3,
        out_specs=[VMEM] * (2 * planes),
        compiler_params=pltpu.CompilerParams(vmem_limit_bytes=SMALL),
        name="combine_rows",
    )(gather_out, gather_in, returned)
    return outs[:planes], outs[planes:]


def cost(flops, arrays):
    return pl.CostEstimate(flops=flops, transcendentals=0, bytes_accessed=sum(2 * a.size for a in arrays))


def chunks(total, body):
    def step(i, carry):
        body(pl.ds(pl.multiple_of(i * CHUNK, CHUNK), CHUNK))
        return carry

    lax.fori_loop(0, total // CHUNK, step, 0)


def join_cores(arrived, joined, side):
    width = arrived.shape[3] // 2
    for core in range(arrived.shape[1]):
        block = arrived[:, core, :, side * width : (side + 1) * width]
        joined[:, core * width : (core + 1) * width] = block.reshape(joined.shape[0], width)


def split_cores(whole, out, side):
    width = out.shape[3] // 2
    for core in range(out.shape[1]):
        block = whole[:, core * width : (core + 1) * width].reshape(out.shape[0], out.shape[2], width)
        out[:, core, :, side * width : (side + 1) * width] = block


def expert_kernel(arrived, *refs):
    sources, (inner_out, back), refs = refs[:6], refs[6:8], refs[8:]
    held, rows, grads, gate_pre, up_pre, whole, out, inner, gate_in, up_in, down_in, sems = refs
    width, middle = gate_in.shape[1] // 2, held.shape[3] // 2
    own, other = slice(0, width), slice(width, 2 * width)
    sides = [(slice(None), slice(None), slice(None), slice(i * middle, (i + 1) * middle)) for i in range(2)]
    fetch = [pltpu.make_async_copy(arrived.at[at], held.at[at], sems.at[6 + i]) for i, at in enumerate(sides)]
    send = [pltpu.make_async_copy(out.at[at], back.at[at], sems.at[8 + i]) for i, at in enumerate(sides)]
    keep = pltpu.make_async_copy(inner, inner_out, sems.at[10])
    fetch[0].start()
    targets = [
        gate_in.at[:, own], gate_in.at[:, other], up_in.at[:, own], up_in.at[:, other], down_in.at[own], down_in.at[other]
    ]
    copies = [
        pltpu.make_async_copy(source, target, sems.at[i])
        for i, (source, target) in enumerate(zip(sources, targets, strict=True))
    ]
    for copy in copies[:2]:
        copy.start()
    fetch[1].start()
    for copy in copies[2:]:
        copy.start()
    fetch[0].wait()
    join_cores(held, rows, 0)
    copies[0].wait()
    copies[1].wait()

    def gate_part(at):
        gate_pre[:, at] = contract(rows[...], gate_in[:, at], ((1,), (0,)))

    chunks(gate_pre.shape[1], gate_part)
    copies[2].wait()
    copies[3].wait()

    def up_part(at):
        up_at = contract(rows[...], up_in[:, at], ((1,), (0,)))
        up_pre[:, at] = up_at
        gate_at = gate_pre[:, at]
        inner[0, :, at] = (gate_at * jax.nn.sigmoid(gate_at) * up_at).astype(inner.dtype)

    chunks(up_pre.shape[1], up_part)
    copies[4].wait()
    copies[5].wait()

    def out_part(at):
        whole[:, at] = contract(inner[0], down_in[:, at], ((1,), (0,))).astype(whole.dtype)

    chunks(whole.shape[1], out_part)
    split_cores(whole, out, 0)
    send[0].start()
    fetch[1].wait()
    join_cores(held, grads, 1)

    def hidden_part(at):
        grad_hidden = contract(grads[...], down_in[at, :], ((1,), (1,)))
        gate_at = gate_pre[:, at]
        sigmoid_gate = jax.nn.sigmoid(gate_at)
        inner[1, :, at] = (
            grad_hidden * up_pre[:, at] * sigmoid_gate * (1.0 + gate_at * (1.0 - sigmoid_gate))
        ).astype(inner.dtype)
        inner[2, :, at] = (grad_hidden * (gate_at * sigmoid_gate)).astype(inner.dtype)

    chunks(gate_pre.shape[1], hidden_part)
    keep.start()

    def in_part(at):
        total = contract(inner[1], gate_in[at, :], ((1,), (1,)))
        total = total + contract(inner[2], up_in[at, :], ((1,), (1,)))
        whole[:, at] = total.astype(whole.dtype)

    chunks(whole.shape[1], in_part)
    split_cores(whole, out, 1)
    send[1].start()
    send[0].wait()
    keep.wait()
    send[1].wait()


def expert(arrived, gate, up, down):
    columns, cores, group, width = arrived.shape
    count, hidden, features = columns * group, cores * gate[0].shape[1], gate[0].shape[0]
    rows, pre = pltpu.VMEM((count, features), jnp.bfloat16), pltpu.VMEM((count, hidden), jnp.float32)
    side, block = pltpu.VMEM((features, hidden), jnp.bfloat16), pltpu.VMEM(arrived.shape, jnp.bfloat16)
    return pl.pallas_call(
        expert_kernel,
        out_shape=[
            jax.ShapeDtypeStruct((3, count, hidden), jnp.bfloat16),
            jax.ShapeDtypeStruct(arrived.shape, jnp.bfloat16),
        ],
        in_specs=[HBM] * 7,
        out_specs=[HBM] * 2,
        scratch_shapes=[
            block, rows, rows, pre, pre, rows, block, pltpu.VMEM((3, count, hidden), jnp.bfloat16), side, side,
            pltpu.VMEM((hidden, features), jnp.bfloat16), pltpu.SemaphoreType.DMA((11,)),
        ],
        compiler_params=pltpu.CompilerParams(vmem_limit_bytes=LARGE),
        cost_estimate=cost(12 * count * hidden * features, [*gate, *up, *down]),
        name="expert",
    )(arrived, *gate, *up, *down)


def weights_kernel(arrived, arrived_other, inner, inner_other, gate_out, up_out, down_out, rows, grads, hidden):
    count, width = inner.shape[1], inner.shape[2] // 2
    for core, block in enumerate((arrived, arrived_other)):
        at = slice(core * count, (core + 1) * count)
        join_cores(block, rows.at[at], 0)
        join_cores(block, grads.at[at], 1)
        for i in range(inner.shape[0]):
            hidden[i, at] = inner_other[i] if core else inner[i, :, :width]

    def by_feature(at):
        part = rows[:, at]
        gate_out[at, :] = contract(part, hidden[1], ((0,), (0,))).astype(gate_out.dtype)
        up_out[at, :] = contract(part, hidden[2], ((0,), (0,))).astype(up_out.dtype)
        down_out[:, at] = contract(hidden[0], grads[:, at], ((0,), (0,))).astype(down_out.dtype)

    chunks(rows.shape[1], by_feature)


def weight_grads(arrived, arrived_other, inner, inner_other):
    columns, cores, group, width = arrived.shape
    count, features, hidden = columns * group, cores * width // 2, inner.shape[2] // 2
    side = jax.ShapeDtypeStruct((features, hidden), jnp.bfloat16)
    rows = pltpu.VMEM((2 * count, features), jnp.bfloat16)
    return pl.pallas_call(
        weights_kernel,
        out_shape=[side, side, jax.ShapeDtypeStruct((hidden, features), jnp.bfloat16)],
        in_specs=[VMEM] * 4,
        out_specs=[VMEM] * 3,
        scratch_shapes=[rows, rows, pltpu.VMEM((3, 2 * count, hidden), jnp.bfloat16)],
        compiler_params=pltpu.CompilerParams(vmem_limit_bytes=MIDDLE),
        cost_estimate=cost(12 * count * hidden * features, [side, side, side]),
        name="weight_grads",
    )(arrived, arrived_other, inner, inner_other)


def on_device(tokens, expert_ids, router_probs, cotangent, w_gate, w_up, w_down):
    planes, columns, cores = lax.axis_size("grp"), lax.axis_size("ep"), lax.axis_size("tp")
    tok_rows, width = tokens.shape
    top_count = expert_ids.shape[1]
    capacity = 3 * tok_rows * top_count // (2 * planes * columns)
    group = planes * capacity // cores
    half_tokens = planes * tok_rows // cores
    me = lax.axis_index("grp")

    routing = jnp.concatenate([expert_ids.T.astype(jnp.float32), router_probs.T], axis=0)
    pieces, routing = ring_gathers([tokens, cotangent], "grp", routing[None])
    routing = jnp.stack([routing[-offset % planes] for offset in ring_offsets(planes)])

    combine = routing[:, top_count:] / jnp.sum(routing[:, top_count:], axis=1, keepdims=True)
    local = routing[:, :top_count] - (me * columns).astype(jnp.float32)
    plane_expert = jnp.arange(columns, dtype=jnp.float32)[:, None, None, None]
    hits = local[None] == plane_expert
    named = jnp.any(hits, axis=2)
    weight = jnp.sum(jnp.where(hits, combine[None], 0.0), axis=2)
    row_at = jnp.arange(tok_rows, dtype=jnp.int32)
    earlier = (row_at[:, None] < row_at[None, :]).astype(jnp.bfloat16)
    rank = contract(
        named.astype(jnp.bfloat16).reshape(columns * planes, tok_rows), earlier, ((1,), (0,))
    ).reshape(columns, planes, tok_rows)
    base = ((jnp.arange(planes) % (planes // cores)) * capacity).astype(jnp.float32)[None, :, None]
    place = jnp.where(named, base + rank, -1.0).reshape(columns, cores, half_tokens)
    weight = weight.reshape(columns, cores, half_tokens)
    slot = jnp.arange(group, dtype=jnp.float32)[None, None, :, None]
    chosen = place.transpose(1, 0, 2)[:, :, None, :] == slot
    select = chosen.astype(jnp.bfloat16).reshape(cores, columns * group, half_tokens)
    slot_weight = jnp.sum(jnp.where(chosen, weight.transpose(1, 0, 2)[:, :, None, :], 0.0), axis=3)
    slot_weight = slot_weight.reshape(cores, columns * group, 1)

    spread = (jnp.arange(columns)[:, None] == jnp.arange(columns * group)[None, :] // group).astype(jnp.bfloat16)
    place_wide = contract(place.transpose(1, 2, 0).astype(jnp.bfloat16), spread, ((2,), (0,)))
    weight_wide = contract(weight.transpose(1, 2, 0).astype(jnp.bfloat16), spread, ((2,), (0,)))
    chosen_back = place_wide == (jnp.arange(columns * group) % group).astype(jnp.float32)[None, None, :]
    gather_in = chosen_back.astype(jnp.bfloat16)
    gather_out = jnp.where(chosen_back, weight_wide, 0.0).astype(jnp.bfloat16)

    shape = (columns, cores, group, 2 * width)

    def exchange(block):
        flat = block.reshape(columns * cores * group, 2 * width)
        return lax.all_to_all(flat, PLANE, split_axis=0, concat_axis=0, tiled=True).reshape(shape)

    def pair(block):
        return block, shift(block, "tp", 1)

    arrived = exchange(pick(select, slot_weight, pieces, shape))
    inner, back = expert(arrived, pair(w_gate[0]), pair(w_up[0]), pair(w_down[0]))
    returned = exchange(back)
    inner_other = shift(inner[:, :, inner.shape[2] // 2 :], "tp", 1)
    weights = weight_grads(*pair(arrived), inner, inner_other)
    returned, grad_gate, grad_up, grad_down = lax.optimization_barrier((returned, *weights))
    parts_out, parts_in = combine_rows(gather_out, gather_in, returned, tok_rows)
    layer_out, grad_tokens = ring_scatter(parts_out, "grp", 0), ring_scatter(parts_in, "grp", 1)
    return (layer_out, grad_tokens, grad_gate[None], grad_up[None], grad_down[None])


def solution(mesh):
    return jax.shard_map(
        on_device,
        mesh=mesh,
        in_specs=(
            P(("grp", "ep"), "tp"),
            P(("grp", "ep"), None),
            P(("grp", "ep"), None),
            P(("grp", "ep"), "tp"),
            P(("grp", "ep"), None, "tp"),
            P(("grp", "ep"), None, "tp"),
            P(("grp", "ep"), "tp", None),
        ),
        out_specs=(
            P(("grp", "ep"), "tp"),
            P(("grp", "ep"), "tp"),
            P(("grp", "ep"), None, "tp"),
            P(("grp", "ep"), None, "tp"),
            P(("grp", "ep"), "tp", None),
        ),
        check_vma=False,
    )
```

```python
import functools

import jax
import jax.numpy as jnp
from jax import lax
from jax.experimental import pallas as pl
from jax.experimental.pallas import tpu as pltpu
from jax.sharding import PartitionSpec as P

PLANE = ("ep", "tp")
VMEM = pl.BlockSpec(memory_space=pltpu.VMEM)
HBM = pl.BlockSpec(memory_space=pl.ANY)
SMALL, MIDDLE, LARGE = 16 << 20, 28 << 20, 56 << 20
CHUNK = 256


def shift(value, axis, distance):
    count = lax.axis_size(axis)
    return lax.ppermute(value, axis, [(i, (i + distance) % count) for i in range(count)])


def ring_offsets(count):
    order = [0]
    for step in range(1, count // 2):
        order += [-step, step]
    return order + [count // 2]


def ring_gathers(blocks, axis, small):
    count = lax.axis_size(axis)
    pieces = [[block] for block in blocks]
    ahead, behind = list(blocks), list(blocks)
    for step in range(1, count // 2):
        for i in range(len(blocks)):
            ahead[i], behind[i] = shift(ahead[i], axis, 1), shift(behind[i], axis, -1)
            pieces[i] += [ahead[i], behind[i]]
        if step == 2:
            small, ahead[0] = lax.optimization_barrier((small, ahead[0]))
    pieces[0].append(shift(ahead[0], axis, 1))
    pieces[1].append(shift(behind[1], axis, -1))
    return pieces[0] + pieces[1], small


def spread_routing(routing, axis):
    blocks = jnp.stack([routing] * lax.axis_size(axis))
    return lax.all_to_all(blocks, axis, split_axis=0, concat_axis=0, tiled=True)


def by_offset(every, axis):
    count = lax.axis_size(axis)
    from_next = lax.dynamic_slice_in_dim(jnp.concatenate([every, every]), lax.axis_index(axis), count, axis=0)
    return jnp.stack([from_next[offset % count] for offset in ring_offsets(count)])


def add_rounded(first, second):
    return (first.astype(jnp.float32) + second.astype(jnp.float32)).astype(jnp.bfloat16)


def ring_scatter(blocks, axis, side):
    count = lax.axis_size(axis)
    where = {offset: i for i, offset in enumerate(ring_offsets(count))}
    sums = [None, None]
    sums[side] = shift(blocks[-1], axis, 1 if side else -1)
    for step in range(count // 2 - 1, 0, -1):
        for way, sign in enumerate((-1, 1)):
            mine = blocks[where[sign * step]]
            total = mine if sums[way] is None else add_rounded(mine, sums[way])
            sums[way] = shift(total, axis, sign)
    return sum(part.astype(jnp.float32) for part in (blocks[0], *sums)).astype(jnp.bfloat16)


def contract(left, right, dims):
    return lax.dot_general(left, right, (dims, ((), ())), preferred_element_type=jnp.float32)


def pick_kernel(select, weight, *refs):
    pieces, (sent, out, sems) = refs[:-3], refs[-3:]
    columns, _, group, width = out.shape
    middle, count = width // 2, len(pieces) // 2
    each, copies = count // select.shape[0], []
    for side in (0, 1):
        whole = [piece[...] for piece in pieces[side * count : (side + 1) * count]]
        for half in range(select.shape[0]):
            source = jnp.concatenate(whole[half * each : (half + 1) * each], axis=0)
            picked = contract(select[half], source, ((1,), (0,)))
            if side:
                picked = picked * weight[half]
            at = slice(side * middle, (side + 1) * middle)
            out[:, half, :, at] = picked.astype(out.dtype).reshape(columns, group, middle)
            copies.append(
                pltpu.make_async_copy(out.at[:, half, :, at], sent.at[:, half, :, at], sems.at[2 * side + half])
            )
            copies[-1].start()
    for copy in copies:
        copy.wait()


def pick(select, weight, pieces, shape):
    return pl.pallas_call(
        pick_kernel,
        out_shape=jax.ShapeDtypeStruct(shape, jnp.bfloat16),
        in_specs=[VMEM] * (2 + len(pieces)),
        out_specs=HBM,
        scratch_shapes=[pltpu.VMEM(shape, jnp.bfloat16), pltpu.SemaphoreType.DMA((4,))],
        compiler_params=pltpu.CompilerParams(vmem_limit_bytes=SMALL),
        name="pick",
    )(select, weight, *pieces)


def combine_kernel(gather_out, gather_in, returned, *outs):
    halves, middle = gather_out.shape[0], returned.shape[3] // 2
    count = len(outs) // 2
    tokens, each = outs[0].shape[0], count // halves
    for side, gather in enumerate((gather_out, gather_in)):
        blocks = outs[side * count : (side + 1) * count]
        for half in range(halves):
            rows = returned[:, half, :, side * middle : (side + 1) * middle].reshape(gather.shape[2], middle)
            total = contract(gather[half], rows, ((1,), (0,))).astype(jnp.bfloat16)
            for i in range(each):
                blocks[half * each + i][...] = total[i * tokens : (i + 1) * tokens]


def combine_rows(gather_out, gather_in, returned, tokens):
    halves, half_tokens, _ = gather_out.shape
    planes, width = halves * half_tokens // tokens, returned.shape[3] // 2
    block = jax.ShapeDtypeStruct((tokens, width), jnp.bfloat16)
    outs = pl.pallas_call(
        combine_kernel,
        out_shape=[block] * (2 * planes),
        in_specs=[VMEM] * 3,
        out_specs=[VMEM] * (2 * planes),
        compiler_params=pltpu.CompilerParams(vmem_limit_bytes=SMALL),
        name="combine_rows",
    )(gather_out, gather_in, returned)
    return outs[:planes], outs[planes:]


def cost(flops, arrays):
    return pl.CostEstimate(flops=flops, transcendentals=0, bytes_accessed=sum(2 * a.size for a in arrays))


def chunks(total, body):
    def step(i, carry):
        body(pl.ds(pl.multiple_of(i * CHUNK, CHUNK), CHUNK))
        return carry

    lax.fori_loop(0, total // CHUNK, step, 0)


def join_cores(arrived, joined, side):
    width = arrived.shape[3] // 2
    for core in range(arrived.shape[1]):
        block = arrived[:, core, :, side * width : (side + 1) * width]
        joined[:, core * width : (core + 1) * width] = block.reshape(joined.shape[0], width)


def split_cores(whole, out, side):
    width = out.shape[3] // 2
    for core in range(out.shape[1]):
        block = whole[:, core * width : (core + 1) * width].reshape(out.shape[0], out.shape[2], width)
        out[:, core, :, side * width : (side + 1) * width] = block


def expert_kernel(arrived, *refs):
    sources, (inner_out, back), refs = refs[:6], refs[6:8], refs[8:]
    held, rows, grads, gate_pre, up_pre, whole, out, inner, gate_in, up_in, down_in, sems = refs
    width, middle = gate_in.shape[1] // 2, held.shape[3] // 2
    own, other = slice(0, width), slice(width, 2 * width)
    sides = [(slice(None), slice(None), slice(None), slice(i * middle, (i + 1) * middle)) for i in range(2)]
    fetch = [pltpu.make_async_copy(arrived.at[at], held.at[at], sems.at[6 + i]) for i, at in enumerate(sides)]
    send = [pltpu.make_async_copy(out.at[at], back.at[at], sems.at[8 + i]) for i, at in enumerate(sides)]
    keep = pltpu.make_async_copy(inner, inner_out, sems.at[10])
    fetch[0].start()
    targets = [
        gate_in.at[:, own], gate_in.at[:, other], up_in.at[:, own], up_in.at[:, other], down_in.at[own], down_in.at[other]
    ]
    copies = [
        pltpu.make_async_copy(source, target, sems.at[i])
        for i, (source, target) in enumerate(zip(sources, targets, strict=True))
    ]
    for copy in copies[:2]:
        copy.start()
    fetch[1].start()
    for copy in copies[2:]:
        copy.start()
    fetch[0].wait()
    join_cores(held, rows, 0)
    copies[0].wait()
    copies[1].wait()

    def gate_part(at):
        gate_pre[:, at] = contract(rows[...], gate_in[:, at], ((1,), (0,)))

    chunks(gate_pre.shape[1], gate_part)
    copies[2].wait()
    copies[3].wait()

    def up_part(at):
        up_at = contract(rows[...], up_in[:, at], ((1,), (0,)))
        up_pre[:, at] = up_at
        gate_at = gate_pre[:, at]
        inner[0, :, at] = (gate_at * jax.nn.sigmoid(gate_at) * up_at).astype(inner.dtype)

    chunks(up_pre.shape[1], up_part)
    copies[4].wait()
    copies[5].wait()

    def out_part(at):
        whole[:, at] = contract(inner[0], down_in[:, at], ((1,), (0,))).astype(whole.dtype)

    chunks(whole.shape[1], out_part)
    split_cores(whole, out, 0)
    send[0].start()
    fetch[1].wait()
    join_cores(held, grads, 1)

    def hidden_part(at):
        grad_hidden = contract(grads[...], down_in[at, :], ((1,), (1,)))
        gate_at = gate_pre[:, at]
        sigmoid_gate = jax.nn.sigmoid(gate_at)
        inner[1, :, at] = (
            grad_hidden * up_pre[:, at] * sigmoid_gate * (1.0 + gate_at * (1.0 - sigmoid_gate))
        ).astype(inner.dtype)
        inner[2, :, at] = (grad_hidden * (gate_at * sigmoid_gate)).astype(inner.dtype)

    chunks(gate_pre.shape[1], hidden_part)
    keep.start()

    def in_part(at):
        total = contract(inner[1], gate_in[at, :], ((1,), (1,)))
        total = total + contract(inner[2], up_in[at, :], ((1,), (1,)))
        whole[:, at] = total.astype(whole.dtype)

    chunks(whole.shape[1], in_part)
    split_cores(whole, out, 1)
    send[1].start()
    send[0].wait()
    keep.wait()
    send[1].wait()


def expert(arrived, gate, up, down):
    columns, cores, group, width = arrived.shape
    count, hidden, features = columns * group, cores * gate[0].shape[1], gate[0].shape[0]
    rows, pre = pltpu.VMEM((count, features), jnp.bfloat16), pltpu.VMEM((count, hidden), jnp.float32)
    side, block = pltpu.VMEM((features, hidden), jnp.bfloat16), pltpu.VMEM(arrived.shape, jnp.bfloat16)
    return pl.pallas_call(
        expert_kernel,
        out_shape=[
            jax.ShapeDtypeStruct((3, count, hidden), jnp.bfloat16),
            jax.ShapeDtypeStruct(arrived.shape, jnp.bfloat16),
        ],
        in_specs=[HBM] * 7,
        out_specs=[HBM] * 2,
        scratch_shapes=[
            block, rows, rows, pre, pre, rows, block, pltpu.VMEM((3, count, hidden), jnp.bfloat16), side, side,
            pltpu.VMEM((hidden, features), jnp.bfloat16), pltpu.SemaphoreType.DMA((11,)),
        ],
        compiler_params=pltpu.CompilerParams(vmem_limit_bytes=LARGE),
        cost_estimate=cost(12 * count * hidden * features, [*gate, *up, *down]),
        name="expert",
    )(arrived, *gate, *up, *down)


def weights_kernel(arrived, arrived_other, inner, inner_other, gate_out, up_out, down_out, rows, grads, hidden):
    count, width = inner.shape[1], inner.shape[2] // 2
    for core, block in enumerate((arrived, arrived_other)):
        at = slice(core * count, (core + 1) * count)
        join_cores(block, rows.at[at], 0)
        join_cores(block, grads.at[at], 1)
        for i in range(inner.shape[0]):
            hidden[i, at] = inner_other[i] if core else inner[i, :, :width]

    def by_feature(at):
        part = rows[:, at]
        gate_out[at, :] = contract(part, hidden[1], ((0,), (0,))).astype(gate_out.dtype)
        up_out[at, :] = contract(part, hidden[2], ((0,), (0,))).astype(up_out.dtype)
        down_out[:, at] = contract(hidden[0], grads[:, at], ((0,), (0,))).astype(down_out.dtype)

    chunks(rows.shape[1], by_feature)


def weight_grads(arrived, arrived_other, inner, inner_other):
    columns, cores, group, width = arrived.shape
    count, features, hidden = columns * group, cores * width // 2, inner.shape[2] // 2
    side = jax.ShapeDtypeStruct((features, hidden), jnp.bfloat16)
    rows = pltpu.VMEM((2 * count, features), jnp.bfloat16)
    return pl.pallas_call(
        weights_kernel,
        out_shape=[side, side, jax.ShapeDtypeStruct((hidden, features), jnp.bfloat16)],
        in_specs=[VMEM] * 4,
        out_specs=[VMEM] * 3,
        scratch_shapes=[rows, rows, pltpu.VMEM((3, 2 * count, hidden), jnp.bfloat16)],
        compiler_params=pltpu.CompilerParams(vmem_limit_bytes=MIDDLE),
        cost_estimate=cost(12 * count * hidden * features, [side, side, side]),
        name="weight_grads",
    )(arrived, arrived_other, inner, inner_other)


def on_device(tokens, expert_ids, router_probs, cotangent, w_gate, w_up, w_down):
    planes, columns, cores = lax.axis_size("grp"), lax.axis_size("ep"), lax.axis_size("tp")
    tok_rows, width = tokens.shape
    top_count = expert_ids.shape[1]
    capacity = 3 * tok_rows * top_count // (2 * planes * columns)
    group = planes * capacity // cores
    half_tokens = planes * tok_rows // cores
    me = lax.axis_index("grp")

    routing = jnp.concatenate([expert_ids.T.astype(jnp.float32), router_probs.T], axis=0)
    pieces, routing = ring_gathers([tokens, cotangent], "grp", spread_routing(routing, "grp"))
    routing = by_offset(routing, "grp")
    combine = routing[:, top_count:] / jnp.sum(routing[:, top_count:], axis=1, keepdims=True)
    local = routing[:, :top_count] - (me * columns).astype(jnp.float32)
    plane_expert = jnp.arange(columns, dtype=jnp.float32)[:, None, None, None]
    hits = local[None] == plane_expert
    named = jnp.any(hits, axis=2)
    weight = jnp.sum(jnp.where(hits, combine[None], 0.0), axis=2)
    row_at = jnp.arange(tok_rows, dtype=jnp.int32)
    earlier = (row_at[:, None] < row_at[None, :]).astype(jnp.bfloat16)
    rank = contract(
        named.astype(jnp.bfloat16).reshape(columns * planes, tok_rows), earlier, ((1,), (0,))
    ).reshape(columns, planes, tok_rows)
    base = ((jnp.arange(planes) % (planes // cores)) * capacity).astype(jnp.float32)[None, :, None]
    place = jnp.where(named, base + rank, -1.0).reshape(columns, cores, half_tokens)
    weight = weight.reshape(columns, cores, half_tokens)
    slot = jnp.arange(group, dtype=jnp.float32)[None, None, :, None]
    chosen = place.transpose(1, 0, 2)[:, :, None, :] == slot
    select = chosen.astype(jnp.bfloat16).reshape(cores, columns * group, half_tokens)
    slot_weight = jnp.sum(jnp.where(chosen, weight.transpose(1, 0, 2)[:, :, None, :], 0.0), axis=3)
    slot_weight = slot_weight.reshape(cores, columns * group, 1)

    shape = (columns, cores, group, 2 * width)

    def exchange(block):
        flat = block.reshape(columns * cores * group, 2 * width)
        return lax.all_to_all(flat, PLANE, split_axis=0, concat_axis=0, tiled=True).reshape(shape)

    def pair(block):
        return block, shift(block, "tp", 1)

    arrived = exchange(pick(select, slot_weight, pieces, shape))
    inner, back = expert(arrived, pair(w_gate[0]), pair(w_up[0]), pair(w_down[0]))
    returned = exchange(back)
    inner_other = shift(inner[:, :, inner.shape[2] // 2 :], "tp", 1)
    weights = weight_grads(*pair(arrived), inner, inner_other)
    place, weight, *weights = lax.optimization_barrier((place, weight, *weights))
    spread = (jnp.arange(columns)[:, None] == jnp.arange(columns * group)[None, :] // group).astype(jnp.bfloat16)
    place_wide = contract(place.transpose(1, 2, 0).astype(jnp.bfloat16), spread, ((2,), (0,)))
    weight_wide = contract(weight.transpose(1, 2, 0).astype(jnp.bfloat16), spread, ((2,), (0,)))
    chosen_back = place_wide == (jnp.arange(columns * group) % group).astype(jnp.float32)[None, None, :]
    gather_in = chosen_back.astype(jnp.bfloat16)
    gather_out = jnp.where(chosen_back, weight_wide, 0.0).astype(jnp.bfloat16)
    returned, gather_in, gather_out, grad_gate, grad_up, grad_down = lax.optimization_barrier(
        (returned, gather_in, gather_out, *weights)
    )
    parts_out, parts_in = combine_rows(gather_out, gather_in, returned, tok_rows)
    layer_out, grad_tokens = ring_scatter(parts_out, "grp", 0), ring_scatter(parts_in, "grp", 1)
    return (layer_out, grad_tokens, grad_gate[None], grad_up[None], grad_down[None])


def solution(mesh):
    return jax.shard_map(
        on_device,
        mesh=mesh,
        in_specs=(
            P(("grp", "ep"), "tp"),
            P(("grp", "ep"), None),
            P(("grp", "ep"), None),
            P(("grp", "ep"), "tp"),
            P(("grp", "ep"), None, "tp"),
            P(("grp", "ep"), None, "tp"),
            P(("grp", "ep"), "tp", None),
        ),
        out_specs=(
            P(("grp", "ep"), "tp"),
            P(("grp", "ep"), "tp"),
            P(("grp", "ep"), None, "tp"),
            P(("grp", "ep"), None, "tp"),
            P(("grp", "ep"), "tp", None),
        ),
        check_vma=False,
    )
```

```python
import functools

import jax
import jax.numpy as jnp
from jax import lax
from jax.experimental import pallas as pl
from jax.experimental.pallas import tpu as pltpu
from jax.sharding import PartitionSpec as P

PLANE = ("ep", "tp")
VMEM = pl.BlockSpec(memory_space=pltpu.VMEM)
HBM = pl.BlockSpec(memory_space=pl.ANY)
SMALL, MIDDLE, LARGE = 16 << 20, 28 << 20, 56 << 20
CHUNK = 256


def shift(value, axis, distance):
    count = lax.axis_size(axis)
    return lax.ppermute(value, axis, [(i, (i + distance) % count) for i in range(count)])


def ring_offsets(count):
    order = [0]
    for step in range(1, count // 2):
        order += [-step, step]
    return order + [count // 2]


def ring_gathers(blocks, axis, small):
    count = lax.axis_size(axis)
    pieces = [[block] for block in blocks]
    ahead, behind = list(blocks), list(blocks)
    for step in range(1, count // 2):
        for i in range(len(blocks)):
            ahead[i], behind[i] = shift(ahead[i], axis, 1), shift(behind[i], axis, -1)
            pieces[i] += [ahead[i], behind[i]]
        if step == 2:
            small, ahead[0] = lax.optimization_barrier((small, ahead[0]))
    pieces[0].append(shift(ahead[0], axis, 1))
    pieces[1].append(shift(behind[1], axis, -1))
    return pieces[0] + pieces[1], small


def spread_routing(routing, axis):
    blocks = jnp.stack([routing] * lax.axis_size(axis))
    return lax.all_to_all(blocks, axis, split_axis=0, concat_axis=0, tiled=True)


def by_offset(every, axis):
    count = lax.axis_size(axis)
    from_next = lax.dynamic_slice_in_dim(jnp.concatenate([every, every]), lax.axis_index(axis), count, axis=0)
    return jnp.stack([from_next[offset % count] for offset in ring_offsets(count)])


def add_rounded(first, second):
    return (first.astype(jnp.float32) + second.astype(jnp.float32)).astype(jnp.bfloat16)


def ring_scatter(blocks, axis, side):
    count = lax.axis_size(axis)
    where = {offset: i for i, offset in enumerate(ring_offsets(count))}
    sums = [None, None]
    sums[side] = shift(blocks[-1], axis, 1 if side else -1)
    for step in range(count // 2 - 1, 0, -1):
        for way, sign in enumerate((-1, 1)):
            mine = blocks[where[sign * step]]
            total = mine if sums[way] is None else add_rounded(mine, sums[way])
            sums[way] = shift(total, axis, sign)
    return sum(part.astype(jnp.float32) for part in (blocks[0], *sums)).astype(jnp.bfloat16)


def contract(left, right, dims):
    return lax.dot_general(left, right, (dims, ((), ())), preferred_element_type=jnp.float32)


def pick_kernel(select, weight, *refs):
    pieces, (sent, out, sems) = refs[:-3], refs[-3:]
    columns, _, group, width = out.shape
    middle, count = width // 2, len(pieces) // 2
    each, copies = count // select.shape[0], []
    for side in (0, 1):
        whole = [piece[...] for piece in pieces[side * count : (side + 1) * count]]
        for half in range(select.shape[0]):
            source = jnp.concatenate(whole[half * each : (half + 1) * each], axis=0)
            picked = contract(select[half], source, ((1,), (0,)))
            if side:
                picked = picked * weight[half]
            at = slice(side * middle, (side + 1) * middle)
            out[:, half, :, at] = picked.astype(out.dtype).reshape(columns, group, middle)
            copies.append(
                pltpu.make_async_copy(out.at[:, half, :, at], sent.at[:, half, :, at], sems.at[2 * side + half])
            )
            copies[-1].start()
    for copy in copies:
        copy.wait()


def pick(select, weight, pieces, shape):
    return pl.pallas_call(
        pick_kernel,
        out_shape=jax.ShapeDtypeStruct(shape, jnp.bfloat16),
        in_specs=[VMEM] * (2 + len(pieces)),
        out_specs=HBM,
        scratch_shapes=[pltpu.VMEM(shape, jnp.bfloat16), pltpu.SemaphoreType.DMA((4,))],
        compiler_params=pltpu.CompilerParams(vmem_limit_bytes=SMALL),
        name="pick",
    )(select, weight, *pieces)


def combine_kernel(gather_out, gather_in, returned, *outs):
    halves, middle = gather_out.shape[0], returned.shape[3] // 2
    count = len(outs) // 2
    tokens, each = outs[0].shape[0], count // halves
    for side, gather in enumerate((gather_out, gather_in)):
        blocks = outs[side * count : (side + 1) * count]
        for half in range(halves):
            rows = returned[:, half, :, side * middle : (side + 1) * middle].reshape(gather.shape[2], middle)
            total = contract(gather[half], rows, ((1,), (0,))).astype(jnp.bfloat16)
            for i in range(each):
                blocks[half * each + i][...] = total[i * tokens : (i + 1) * tokens]


def combine_rows(gather_out, gather_in, returned, tokens):
    halves, half_tokens, _ = gather_out.shape
    planes, width = halves * half_tokens // tokens, returned.shape[3] // 2
    block = jax.ShapeDtypeStruct((tokens, width), jnp.bfloat16)
    outs = pl.pallas_call(
        combine_kernel,
        out_shape=[block] * (2 * planes),
        in_specs=[VMEM] * 3,
        out_specs=[VMEM] * (2 * planes),
        compiler_params=pltpu.CompilerParams(vmem_limit_bytes=SMALL),
        name="combine_rows",
    )(gather_out, gather_in, returned)
    return outs[:planes], outs[planes:]


def cost(flops, arrays):
    return pl.CostEstimate(flops=flops, transcendentals=0, bytes_accessed=sum(2 * a.size for a in arrays))


def chunks(total, body, size=CHUNK):
    def step(i, carry):
        body(pl.ds(pl.multiple_of(i * size, size), size))
        return carry

    lax.fori_loop(0, total // size, step, 0)


def join_cores(arrived, joined, side):
    width = arrived.shape[3] // 2
    for core in range(arrived.shape[1]):
        block = arrived[:, core, :, side * width : (side + 1) * width]
        joined[:, core * width : (core + 1) * width] = block.reshape(joined.shape[0], width)


def expert_kernel(arrived, *refs):
    sources, (inner_out, back), refs = refs[:6], refs[6:8], refs[8:]
    held, rows, grads, out, inner, gate_in, up_in, down_in, sems = refs
    width, features = gate_in.shape[1] // 2, held.shape[3] // 2
    columns, cores, group, _ = held.shape
    own, other = slice(0, width), slice(width, 2 * width)
    targets = [
        gate_in.at[:, own], gate_in.at[:, other], up_in.at[:, own], up_in.at[:, other], down_in.at[own], down_in.at[other]
    ]
    copies = [
        pltpu.make_async_copy(source, target, sems.at[i])
        for i, (source, target) in enumerate(zip(sources, targets, strict=True))
    ]
    fetch = pltpu.make_async_copy(arrived, held, sems.at[6])
    keep = pltpu.make_async_copy(inner, inner_out, sems.at[7])
    send = pltpu.make_async_copy(out, back, sems.at[8])
    fetch.start()
    for copy in copies[0::2] + copies[1::2]:
        copy.start()
    fetch.wait()
    join_cores(held, rows, 0)
    join_cores(held, grads, 1)
    for copy in copies[0::2]:
        copy.wait()

    def hidden_part(at):
        @pl.when(at.start == CHUNK)
        def _():
            for copy in copies[1::2]:
                copy.wait()

        gate_at = contract(rows[...], gate_in[:, at], ((1,), (0,)))
        up_at = contract(rows[...], up_in[:, at], ((1,), (0,)))
        grad_hidden = contract(grads[...], down_in[at, :], ((1,), (1,)))
        sigmoid_gate = jax.nn.sigmoid(gate_at)
        activated = gate_at * sigmoid_gate
        inner[0, :, at] = (activated * up_at).astype(inner.dtype)
        inner[1, :, at] = (
            grad_hidden * up_at * sigmoid_gate * (1.0 + gate_at * (1.0 - sigmoid_gate))
        ).astype(inner.dtype)
        inner[2, :, at] = (grad_hidden * activated).astype(inner.dtype)

    chunks(2 * width, hidden_part)
    keep.start()

    def out_part(at):
        core = at.start // features
        inside = at.start - core * features
        out_at = contract(inner[0], down_in[:, at], ((1,), (0,)))
        in_at = contract(inner[1], gate_in[at, :], ((1,), (1,))) + contract(inner[2], up_in[at, :], ((1,), (1,)))
        for side, total in enumerate((out_at, in_at)):
            to = pl.ds(pl.multiple_of(inside + side * features, CHUNK), 2 * CHUNK)
            out[:, core, :, to] = total.astype(out.dtype).reshape(columns, group, 2 * CHUNK)

    chunks(cores * features, out_part, 2 * CHUNK)
    send.start()
    keep.wait()
    send.wait()


def expert(arrived, gate, up, down):
    columns, cores, group, width = arrived.shape
    count, hidden, features = columns * group, cores * gate[0].shape[1], gate[0].shape[0]
    rows = pltpu.VMEM((count, features), jnp.bfloat16)
    side, block = pltpu.VMEM((features, hidden), jnp.bfloat16), pltpu.VMEM(arrived.shape, jnp.bfloat16)
    return pl.pallas_call(
        expert_kernel,
        out_shape=[
            jax.ShapeDtypeStruct((3, count, hidden), jnp.bfloat16),
            jax.ShapeDtypeStruct(arrived.shape, jnp.bfloat16),
        ],
        in_specs=[HBM] * 7,
        out_specs=[HBM] * 2,
        scratch_shapes=[
            block, rows, rows, block, pltpu.VMEM((3, count, hidden), jnp.bfloat16), side, side,
            pltpu.VMEM((hidden, features), jnp.bfloat16), pltpu.SemaphoreType.DMA((9,)),
        ],
        compiler_params=pltpu.CompilerParams(vmem_limit_bytes=LARGE),
        cost_estimate=cost(12 * count * hidden * features, [*gate, *up, *down]),
        name="expert",
    )(arrived, *gate, *up, *down)


def weights_kernel(arrived, arrived_other, inner, inner_other, gate_out, up_out, down_out, rows, grads, hidden):
    count, width = inner.shape[1], inner.shape[2] // 2
    for core, block in enumerate((arrived, arrived_other)):
        at = slice(core * count, (core + 1) * count)
        join_cores(block, rows.at[at], 0)
        join_cores(block, grads.at[at], 1)
        for i in range(inner.shape[0]):
            hidden[i, at] = inner_other[i] if core else inner[i, :, :width]

    def by_feature(at):
        part = rows[:, at]
        gate_out[at, :] = contract(part, hidden[1], ((0,), (0,))).astype(gate_out.dtype)
        up_out[at, :] = contract(part, hidden[2], ((0,), (0,))).astype(up_out.dtype)
        down_out[:, at] = contract(hidden[0], grads[:, at], ((0,), (0,))).astype(down_out.dtype)

    chunks(rows.shape[1], by_feature)


def weight_grads(arrived, arrived_other, inner, inner_other):
    columns, cores, group, width = arrived.shape
    count, features, hidden = columns * group, cores * width // 2, inner.shape[2] // 2
    side = jax.ShapeDtypeStruct((features, hidden), jnp.bfloat16)
    rows = pltpu.VMEM((2 * count, features), jnp.bfloat16)
    return pl.pallas_call(
        weights_kernel,
        out_shape=[side, side, jax.ShapeDtypeStruct((hidden, features), jnp.bfloat16)],
        in_specs=[VMEM] * 4,
        out_specs=[VMEM] * 3,
        scratch_shapes=[rows, rows, pltpu.VMEM((3, 2 * count, hidden), jnp.bfloat16)],
        compiler_params=pltpu.CompilerParams(vmem_limit_bytes=MIDDLE),
        cost_estimate=cost(12 * count * hidden * features, [side, side, side]),
        name="weight_grads",
    )(arrived, arrived_other, inner, inner_other)


def on_device(tokens, expert_ids, router_probs, cotangent, w_gate, w_up, w_down):
    planes, columns, cores = lax.axis_size("grp"), lax.axis_size("ep"), lax.axis_size("tp")
    tok_rows, width = tokens.shape
    top_count = expert_ids.shape[1]
    capacity = 3 * tok_rows * top_count // (2 * planes * columns)
    group = planes * capacity // cores
    half_tokens = planes * tok_rows // cores
    me = lax.axis_index("grp")

    routing = jnp.concatenate([expert_ids.T.astype(jnp.float32), router_probs.T], axis=0)
    pieces, routing = ring_gathers([tokens, cotangent], "grp", spread_routing(routing, "grp"))
    routing = by_offset(routing, "grp")
    combine = routing[:, top_count:] / jnp.sum(routing[:, top_count:], axis=1, keepdims=True)
    local = routing[:, :top_count] - (me * columns).astype(jnp.float32)
    plane_expert = jnp.arange(columns, dtype=jnp.float32)[:, None, None, None]
    hits = local[None] == plane_expert
    named = jnp.any(hits, axis=2)
    weight = jnp.sum(jnp.where(hits, combine[None], 0.0), axis=2)
    row_at = jnp.arange(tok_rows, dtype=jnp.int32)
    earlier = (row_at[:, None] < row_at[None, :]).astype(jnp.bfloat16)
    rank = contract(
        named.astype(jnp.bfloat16).reshape(columns * planes, tok_rows), earlier, ((1,), (0,))
    ).reshape(columns, planes, tok_rows)
    base = ((jnp.arange(planes) % (planes // cores)) * capacity).astype(jnp.float32)[None, :, None]
    place = jnp.where(named, base + rank, -1.0).reshape(columns, cores, half_tokens)
    weight = weight.reshape(columns, cores, half_tokens)
    slot = jnp.arange(group, dtype=jnp.float32)[None, None, :, None]
    chosen = place.transpose(1, 0, 2)[:, :, None, :] == slot
    select = chosen.astype(jnp.bfloat16).reshape(cores, columns * group, half_tokens)
    slot_weight = jnp.sum(jnp.where(chosen, weight.transpose(1, 0, 2)[:, :, None, :], 0.0), axis=3)
    slot_weight = slot_weight.reshape(cores, columns * group, 1)

    shape = (columns, cores, group, 2 * width)

    def exchange(block):
        flat = block.reshape(columns * cores * group, 2 * width)
        return lax.all_to_all(flat, PLANE, split_axis=0, concat_axis=0, tiled=True).reshape(shape)

    def pair(block):
        return block, shift(block, "tp", 1)

    arrived = exchange(pick(select, slot_weight, pieces, shape))
    inner, back = expert(arrived, pair(w_gate[0]), pair(w_up[0]), pair(w_down[0]))
    returned = exchange(back)
    inner_other = shift(inner[:, :, inner.shape[2] // 2 :], "tp", 1)
    weights = weight_grads(*pair(arrived), inner, inner_other)
    place, weight, *weights = lax.optimization_barrier((place, weight, *weights))
    spread = (jnp.arange(columns)[:, None] == jnp.arange(columns * group)[None, :] // group).astype(jnp.bfloat16)
    place_wide = contract(place.transpose(1, 2, 0).astype(jnp.bfloat16), spread, ((2,), (0,)))
    weight_wide = contract(weight.transpose(1, 2, 0).astype(jnp.bfloat16), spread, ((2,), (0,)))
    chosen_back = place_wide == (jnp.arange(columns * group) % group).astype(jnp.float32)[None, None, :]
    gather_in = chosen_back.astype(jnp.bfloat16)
    gather_out = jnp.where(chosen_back, weight_wide, 0.0).astype(jnp.bfloat16)
    returned, gather_in, gather_out, grad_gate, grad_up, grad_down = lax.optimization_barrier(
        (returned, gather_in, gather_out, *weights)
    )
    parts_out, parts_in = combine_rows(gather_out, gather_in, returned, tok_rows)
    layer_out, grad_tokens = ring_scatter(parts_out, "grp", 0), ring_scatter(parts_in, "grp", 1)
    return (layer_out, grad_tokens, grad_gate[None], grad_up[None], grad_down[None])


def solution(mesh):
    return jax.shard_map(
        on_device,
        mesh=mesh,
        in_specs=(
            P(("grp", "ep"), "tp"),
            P(("grp", "ep"), None),
            P(("grp", "ep"), None),
            P(("grp", "ep"), "tp"),
            P(("grp", "ep"), None, "tp"),
            P(("grp", "ep"), None, "tp"),
            P(("grp", "ep"), "tp", None),
        ),
        out_specs=(
            P(("grp", "ep"), "tp"),
            P(("grp", "ep"), "tp"),
            P(("grp", "ep"), None, "tp"),
            P(("grp", "ep"), None, "tp"),
            P(("grp", "ep"), "tp", None),
        ),
        check_vma=False,
    )
```

```python
import functools

import jax
import jax.numpy as jnp
from jax import lax
from jax.experimental import pallas as pl
from jax.experimental.pallas import tpu as pltpu
from jax.sharding import PartitionSpec as P

PLANE = ("ep", "tp")
VMEM = pl.BlockSpec(memory_space=pltpu.VMEM)
HBM = pl.BlockSpec(memory_space=pl.ANY)
SMALL, MIDDLE, LARGE = 16 << 20, 28 << 20, 56 << 20
CHUNK = 256


def shift(value, axis, distance):
    count = lax.axis_size(axis)
    return lax.ppermute(value, axis, [(i, (i + distance) % count) for i in range(count)])


def ring_offsets(count):
    order = [0]
    for step in range(1, count // 2):
        order += [-step, step]
    return order + [count // 2]


def ring_gathers(blocks, axis, small):
    count = lax.axis_size(axis)
    pieces = [[block] for block in blocks]
    ahead, behind = list(blocks), list(blocks)
    for step in range(1, count // 2):
        for i in range(len(blocks)):
            ahead[i], behind[i] = shift(ahead[i], axis, 1), shift(behind[i], axis, -1)
            pieces[i] += [ahead[i], behind[i]]
        if step == 2:
            small, ahead[0] = lax.optimization_barrier((small, ahead[0]))
    pieces[0].append(shift(ahead[0], axis, 1))
    pieces[1].append(shift(behind[1], axis, -1))
    return pieces[0] + pieces[1], small


def spread_routing(routing, axis):
    blocks = jnp.stack([routing] * lax.axis_size(axis))
    return lax.all_to_all(blocks, axis, split_axis=0, concat_axis=0, tiled=True)


def by_offset(every, axis):
    count = lax.axis_size(axis)
    from_next = lax.dynamic_slice_in_dim(jnp.concatenate([every, every]), lax.axis_index(axis), count, axis=0)
    return jnp.stack([from_next[offset % count] for offset in ring_offsets(count)])


def add_rounded(first, second):
    return (first.astype(jnp.float32) + second.astype(jnp.float32)).astype(jnp.bfloat16)


def ring_scatter(blocks, axis, side):
    count = lax.axis_size(axis)
    where = {offset: i for i, offset in enumerate(ring_offsets(count))}
    sums = [None, None]
    sums[side] = shift(blocks[-1], axis, 1 if side else -1)
    for step in range(count // 2 - 1, 0, -1):
        for way, sign in enumerate((-1, 1)):
            mine = blocks[where[sign * step]]
            total = mine if sums[way] is None else add_rounded(mine, sums[way])
            sums[way] = shift(total, axis, sign)
    return sum(part.astype(jnp.float32) for part in (blocks[0], *sums)).astype(jnp.bfloat16)


def contract(left, right, dims):
    return lax.dot_general(left, right, (dims, ((), ())), preferred_element_type=jnp.float32)


def pick_kernel(select, weight, *refs):
    pieces, (sent, out, sems) = refs[:-3], refs[-3:]
    columns, _, group, width = out.shape
    middle, count = width // 2, len(pieces) // 2
    each, copies = count // select.shape[0], []
    for side in (0, 1):
        whole = [piece[...] for piece in pieces[side * count : (side + 1) * count]]
        for half in range(select.shape[0]):
            source = jnp.concatenate(whole[half * each : (half + 1) * each], axis=0)
            picked = contract(select[half], source, ((1,), (0,)))
            if side:
                picked = picked * weight[half]
            at = slice(side * middle, (side + 1) * middle)
            out[:, half, :, at] = picked.astype(out.dtype).reshape(columns, group, middle)
            copies.append(
                pltpu.make_async_copy(out.at[:, half, :, at], sent.at[:, half, :, at], sems.at[2 * side + half])
            )
            copies[-1].start()
    for copy in copies:
        copy.wait()


def pick(select, weight, pieces, shape):
    return pl.pallas_call(
        pick_kernel,
        out_shape=jax.ShapeDtypeStruct(shape, jnp.bfloat16),
        in_specs=[VMEM] * (2 + len(pieces)),
        out_specs=HBM,
        scratch_shapes=[pltpu.VMEM(shape, jnp.bfloat16), pltpu.SemaphoreType.DMA((4,))],
        compiler_params=pltpu.CompilerParams(vmem_limit_bytes=SMALL),
        name="pick",
    )(select, weight, *pieces)


def combine_kernel(place, weight, spread, within, returned, *outs):
    halves, middle = place.shape[0], returned.shape[3] // 2
    count = len(outs) // 2
    tokens, each = outs[0].shape[0], count // halves
    for half in range(halves):
        chosen = contract(place[half], spread[...], ((0,), (0,))) == within[...]
        heavy = jnp.where(chosen, contract(weight[half], spread[...], ((0,), (0,))), 0.0)
        for side, gather in enumerate((heavy, jnp.where(chosen, 1.0, 0.0))):
            blocks = outs[side * count : (side + 1) * count]
            rows = returned[:, half, :, side * middle : (side + 1) * middle].reshape(gather.shape[1], middle)
            total = contract(gather.astype(jnp.bfloat16), rows, ((1,), (0,))).astype(jnp.bfloat16)
            for i in range(each):
                blocks[half * each + i][...] = total[i * tokens : (i + 1) * tokens]


def combine_rows(place, weight, spread, within, returned, tokens):
    halves, _, half_tokens = place.shape
    planes, width = halves * half_tokens // tokens, returned.shape[3] // 2
    block = jax.ShapeDtypeStruct((tokens, width), jnp.bfloat16)
    outs = pl.pallas_call(
        combine_kernel,
        out_shape=[block] * (2 * planes),
        in_specs=[VMEM] * 5,
        out_specs=[VMEM] * (2 * planes),
        compiler_params=pltpu.CompilerParams(vmem_limit_bytes=SMALL),
        name="combine_rows",
    )(place, weight, spread, within, returned)
    return outs[:planes], outs[planes:]


def cost(flops, arrays):
    return pl.CostEstimate(flops=flops, transcendentals=0, bytes_accessed=sum(2 * a.size for a in arrays))


def chunks(total, body, size=CHUNK):
    def step(i, carry):
        body(pl.ds(pl.multiple_of(i * size, size), size))
        return carry

    lax.fori_loop(0, total // size, step, 0)


def join_cores(arrived, joined, side):
    width = arrived.shape[3] // 2
    for core in range(arrived.shape[1]):
        block = arrived[:, core, :, side * width : (side + 1) * width]
        joined[:, core * width : (core + 1) * width] = block.reshape(joined.shape[0], width)


def expert_kernel(arrived, *refs):
    sources, (inner_out, back), refs = refs[:6], refs[6:8], refs[8:]
    held, rows, grads, out, inner, gate_in, up_in, down_in, sems = refs
    width, features = gate_in.shape[1] // 2, held.shape[3] // 2
    columns, cores, group, _ = held.shape
    own, other = slice(0, width), slice(width, 2 * width)
    targets = [
        gate_in.at[:, own], gate_in.at[:, other], up_in.at[:, own], up_in.at[:, other], down_in.at[own], down_in.at[other]
    ]
    copies = [
        pltpu.make_async_copy(source, target, sems.at[i])
        for i, (source, target) in enumerate(zip(sources, targets, strict=True))
    ]
    fetch = pltpu.make_async_copy(arrived, held, sems.at[6])
    keep = pltpu.make_async_copy(inner, inner_out, sems.at[7])
    send = pltpu.make_async_copy(out, back, sems.at[8])
    fetch.start()
    for copy in copies[0::2] + copies[1::2]:
        copy.start()
    fetch.wait()
    join_cores(held, rows, 0)
    join_cores(held, grads, 1)
    for copy in copies[0::2]:
        copy.wait()

    def hidden_part(at):
        @pl.when(at.start == CHUNK)
        def _():
            for copy in copies[1::2]:
                copy.wait()

        gate_at = contract(rows[...], gate_in[:, at], ((1,), (0,)))
        up_at = contract(rows[...], up_in[:, at], ((1,), (0,)))
        grad_hidden = contract(grads[...], down_in[at, :], ((1,), (1,)))
        sigmoid_gate = jax.nn.sigmoid(gate_at)
        activated = gate_at * sigmoid_gate
        inner[0, :, at] = (activated * up_at).astype(inner.dtype)
        inner[1, :, at] = (
            grad_hidden * up_at * sigmoid_gate * (1.0 + gate_at * (1.0 - sigmoid_gate))
        ).astype(inner.dtype)
        inner[2, :, at] = (grad_hidden * activated).astype(inner.dtype)

    chunks(2 * width, hidden_part)
    keep.start()

    def out_part(at):
        core = at.start // features
        inside = at.start - core * features
        out_at = contract(inner[0], down_in[:, at], ((1,), (0,)))
        in_at = contract(inner[1], gate_in[at, :], ((1,), (1,))) + contract(inner[2], up_in[at, :], ((1,), (1,)))
        for side, total in enumerate((out_at, in_at)):
            to = pl.ds(pl.multiple_of(inside + side * features, CHUNK), 2 * CHUNK)
            out[:, core, :, to] = total.astype(out.dtype).reshape(columns, group, 2 * CHUNK)

    chunks(cores * features, out_part, 2 * CHUNK)
    send.start()
    keep.wait()
    send.wait()


def expert(arrived, gate, up, down):
    columns, cores, group, width = arrived.shape
    count, hidden, features = columns * group, cores * gate[0].shape[1], gate[0].shape[0]
    rows = pltpu.VMEM((count, features), jnp.bfloat16)
    side, block = pltpu.VMEM((features, hidden), jnp.bfloat16), pltpu.VMEM(arrived.shape, jnp.bfloat16)
    return pl.pallas_call(
        expert_kernel,
        out_shape=[
            jax.ShapeDtypeStruct((3, count, hidden), jnp.bfloat16),
            jax.ShapeDtypeStruct(arrived.shape, jnp.bfloat16),
        ],
        in_specs=[HBM] * 7,
        out_specs=[HBM] * 2,
        scratch_shapes=[
            block, rows, rows, block, pltpu.VMEM((3, count, hidden), jnp.bfloat16), side, side,
            pltpu.VMEM((hidden, features), jnp.bfloat16), pltpu.SemaphoreType.DMA((9,)),
        ],
        compiler_params=pltpu.CompilerParams(vmem_limit_bytes=LARGE),
        cost_estimate=cost(12 * count * hidden * features, [*gate, *up, *down]),
        name="expert",
    )(arrived, *gate, *up, *down)


def weights_kernel(arrived, arrived_other, inner, inner_other, gate_out, up_out, down_out, rows, grads, hidden):
    count, width = inner.shape[1], inner.shape[2] // 2
    for core, block in enumerate((arrived, arrived_other)):
        at = slice(core * count, (core + 1) * count)
        join_cores(block, rows.at[at], 0)
        join_cores(block, grads.at[at], 1)
        for i in range(inner.shape[0]):
            hidden[i, at] = inner_other[i] if core else inner[i, :, :width]

    def by_feature(at):
        part = rows[:, at]
        gate_out[at, :] = contract(part, hidden[1], ((0,), (0,))).astype(gate_out.dtype)
        up_out[at, :] = contract(part, hidden[2], ((0,), (0,))).astype(up_out.dtype)
        down_out[:, at] = contract(hidden[0], grads[:, at], ((0,), (0,))).astype(down_out.dtype)

    chunks(rows.shape[1], by_feature)


def weight_grads(arrived, arrived_other, inner, inner_other):
    columns, cores, group, width = arrived.shape
    count, features, hidden = columns * group, cores * width // 2, inner.shape[2] // 2
    side = jax.ShapeDtypeStruct((features, hidden), jnp.bfloat16)
    rows = pltpu.VMEM((2 * count, features), jnp.bfloat16)
    return pl.pallas_call(
        weights_kernel,
        out_shape=[side, side, jax.ShapeDtypeStruct((hidden, features), jnp.bfloat16)],
        in_specs=[VMEM] * 4,
        out_specs=[VMEM] * 3,
        scratch_shapes=[rows, rows, pltpu.VMEM((3, 2 * count, hidden), jnp.bfloat16)],
        compiler_params=pltpu.CompilerParams(vmem_limit_bytes=MIDDLE),
        cost_estimate=cost(12 * count * hidden * features, [side, side, side]),
        name="weight_grads",
    )(arrived, arrived_other, inner, inner_other)


def on_device(tokens, expert_ids, router_probs, cotangent, w_gate, w_up, w_down):
    planes, columns, cores = lax.axis_size("grp"), lax.axis_size("ep"), lax.axis_size("tp")
    tok_rows, width = tokens.shape
    top_count = expert_ids.shape[1]
    capacity = 3 * tok_rows * top_count // (2 * planes * columns)
    group = planes * capacity // cores
    half_tokens = planes * tok_rows // cores
    me = lax.axis_index("grp")

    routing = jnp.concatenate([expert_ids.T.astype(jnp.float32), router_probs.T], axis=0)
    pieces, routing = ring_gathers([tokens, cotangent], "grp", spread_routing(routing, "grp"))
    routing = by_offset(routing, "grp")
    combine = routing[:, top_count:] / jnp.sum(routing[:, top_count:], axis=1, keepdims=True)
    local = routing[:, :top_count] - (me * columns).astype(jnp.float32)
    plane_expert = jnp.arange(columns, dtype=jnp.float32)[:, None, None, None]
    hits = local[None] == plane_expert
    named = jnp.any(hits, axis=2)
    weight = jnp.sum(jnp.where(hits, combine[None], 0.0), axis=2)
    row_at = jnp.arange(tok_rows, dtype=jnp.int32)
    earlier = (row_at[:, None] < row_at[None, :]).astype(jnp.bfloat16)
    rank = contract(
        named.astype(jnp.bfloat16).reshape(columns * planes, tok_rows), earlier, ((1,), (0,))
    ).reshape(columns, planes, tok_rows)
    base = ((jnp.arange(planes) % (planes // cores)) * capacity).astype(jnp.float32)[None, :, None]
    place = jnp.where(named, base + rank, -1.0).reshape(columns, cores, half_tokens)
    weight = weight.reshape(columns, cores, half_tokens)
    slot = jnp.arange(group, dtype=jnp.float32)[None, None, :, None]
    chosen = place.transpose(1, 0, 2)[:, :, None, :] == slot
    select = chosen.astype(jnp.bfloat16).reshape(cores, columns * group, half_tokens)
    slot_weight = jnp.sum(jnp.where(chosen, weight.transpose(1, 0, 2)[:, :, None, :], 0.0), axis=3)
    slot_weight = slot_weight.reshape(cores, columns * group, 1)

    shape = (columns, cores, group, 2 * width)

    def exchange(block):
        flat = block.reshape(columns * cores * group, 2 * width)
        return lax.all_to_all(flat, PLANE, split_axis=0, concat_axis=0, tiled=True).reshape(shape)

    def pair(block):
        return block, shift(block, "tp", 1)

    arrived = exchange(pick(select, slot_weight, pieces, shape))
    inner, back = expert(arrived, pair(w_gate[0]), pair(w_up[0]), pair(w_down[0]))
    returned = exchange(back)
    inner_other = shift(inner[:, :, inner.shape[2] // 2 :], "tp", 1)
    weights = weight_grads(*pair(arrived), inner, inner_other)
    place, weight, *weights = lax.optimization_barrier((place, weight, *weights))
    spread = (jnp.arange(columns)[:, None] == jnp.arange(columns * group)[None, :] // group).astype(jnp.bfloat16)
    within = (jnp.arange(columns * group) % group).astype(jnp.float32)[None, :]
    place_by_half = place.transpose(1, 0, 2).astype(jnp.bfloat16)
    weight_by_half = weight.transpose(1, 0, 2).astype(jnp.bfloat16)
    returned, place_by_half, weight_by_half, grad_gate, grad_up, grad_down = lax.optimization_barrier(
        (returned, place_by_half, weight_by_half, *weights)
    )
    parts_out, parts_in = combine_rows(place_by_half, weight_by_half, spread, within, returned, tok_rows)
    layer_out, grad_tokens = ring_scatter(parts_out, "grp", 0), ring_scatter(parts_in, "grp", 1)
    return (layer_out, grad_tokens, grad_gate[None], grad_up[None], grad_down[None])


def solution(mesh):
    return jax.shard_map(
        on_device,
        mesh=mesh,
        in_specs=(
            P(("grp", "ep"), "tp"),
            P(("grp", "ep"), None),
            P(("grp", "ep"), None),
            P(("grp", "ep"), "tp"),
            P(("grp", "ep"), None, "tp"),
            P(("grp", "ep"), None, "tp"),
            P(("grp", "ep"), "tp", None),
        ),
        out_specs=(
            P(("grp", "ep"), "tp"),
            P(("grp", "ep"), "tp"),
            P(("grp", "ep"), None, "tp"),
            P(("grp", "ep"), None, "tp"),
            P(("grp", "ep"), "tp", None),
        ),
        check_vma=False,
    )
```
